1024 devices in a mesh: gx: 32 (over z, core), gy: 4 (over x), gz: 8 (over y).
Axes of the slice: x: 4, y: 8, z: 16, core: 2. Of those that a mesh axis runs over, the one named last changes fastest.
Arguments:
- conductivity: float32 [128, 256, 512], P('gx', 'gz', 'gy'), may hold values from 0.2 to 5
- initial_guess: float32 [128, 256, 512], P('gx', 'gz', 'gy'), may hold values from -6 to 6
- right_side: float32 [128, 256, 512], P('gx', 'gz', 'gy')
Outputs:
- fine_solution: float32 [128, 256, 512], P('gx', 'gz', 'gy')
- level_one_solution: float32 [64, 128, 256], P('gx', 'gz', 'gy')
- level_two_solution: float32 [32, 64, 128], P(None, 'gz', 'gy')
- level_three_solution: float32 [16, 32, 64], P(None, 'gz', 'gy')
- level_three_residual: float32 [16, 32, 64], P(None, 'gz', 'gy')
The draws below stay inside these ranges and needn't reach their ends.
All inputs are finite; a program needn't handle non-finite values.
Results may differ from the reference program's by a relative error of at most 0.000034.
Values sent between devices are 32-bit elements; how exact they have to be, the bound alone decides.
No kernel may reach another device: no remote copies, remote signals or barrier semaphores. Data moves between devices by JAX's collectives and lax.ppermute only.
A program may use at most 32 MiB of HBM per device.

```python
import math
import jax
import jax.numpy as jnp

SWEEPS = 3
NX = 128
NZ = 256
NY = 512


def draw_right_side(key, part):
    rough = jax.random.normal(key, (NX, NZ, NY), jnp.float32)
    rough = jnp.clip(rough, -6.0, 6.0)
    return rough


def block_scale(rng, dims, pieces, smallest, high):
    gain, own = 1.0, jax.random.fold_in(rng, 6)
    for position, shards_of in pieces:
        draws = jnp.exp(jax.random.uniform(jax.random.fold_in(own, position), (shards_of,), jnp.float32, smallest / len(pieces), high / len(pieces)))
        gain = gain * jnp.repeat(draws, dims[position] // shards_of).reshape([-1 if axis == position else 1 for axis in range(len(dims))])
    return gain


def normal_values(own_key, dims, scale, most, shards=(), kind=jnp.bfloat16):
    entries = jax.random.normal(own_key, dims, jnp.float32) * scale
    if len(shards) > 0:
        entries = block_scale(own_key, dims, shards, -0.22, 0.18) * entries
    return jnp.clip(entries, min=-most, max=most).astype(kind)


def setup_inputs(seed: int = 0) -> dict:
    key_list = jax.random.split(jax.random.key(seed), 4)
    return {
        "conductivity": jnp.clip(jnp.exp(math.log(5.0) - 3.218876 * jax.random.uniform(key_list[0], (NX, NZ, NY), jnp.float32) ** block_scale(key_list[0], (NX, NZ, NY), ((0, 32), (1, 8), (2, 4)), -0.2, 0.2)), 0.2, 5.0),
        "initial_guess": normal_values(key_list[1], (NX, NZ, NY), 1.0, 6.0, ((0, 32), (1, 8), (2, 4)), jnp.float32),
        "right_side": draw_right_side(jax.random.fold_in(key_list[3], 71), 0),
    }


lower_bound = 0.25
upper_bound = 2.0


def neighbours(padded):
    return [padded[:-2, 1:-1, 1:-1], padded[2:, 1:-1, 1:-1],
            padded[1:-1, :-2, 1:-1], padded[1:-1, 2:, 1:-1],
            padded[1:-1, 1:-1, :-2], padded[1:-1, 1:-1, 2:]]


def face_terms(conduct):
    others = neighbours(jnp.pad(conduct, 1))
    weights = [0.5 * (conduct + other) for other in others]
    diagonal = weights[0] + weights[1] + weights[2] + weights[3] + weights[4] + weights[5]
    return weights, diagonal


def operate(field, weights, diagonal):
    others = neighbours(jnp.pad(field, 1))
    result = diagonal * field
    for face_index in range(6):
        result = result - weights[face_index] * others[face_index]
    return result


def smooth(source, start, conduct):
    theta = 0.5 * (upper_bound + lower_bound)
    delta = 0.5 * (upper_bound - lower_bound)
    sigma = theta / delta
    weights, diagonal = face_terms(conduct)
    if start is None:
        solution = jnp.zeros_like(source)
        residual = source
    else:
        solution = start
        residual = source - operate(start, weights, diagonal)
    direction = residual / (theta * diagonal)
    ratio_now = 1.0 / sigma
    for sweep_index in range(SWEEPS):
        solution = solution + direction
        residual = residual - operate(direction, weights, diagonal)
        if sweep_index + 1 < SWEEPS:
            ratio_next = 1.0 / (2.0 * sigma - ratio_now)
            direction = (ratio_next * ratio_now) * direction + (2.0 * ratio_next / delta) * residual / diagonal
            ratio_now = ratio_next
    return solution, residual


def coarse_sum(field):
    first, second, third = field.shape
    blocks = field.reshape(first // 2, 2, second // 2, 2, third // 2, 2)
    return jnp.sum(blocks, axis=(1, 3, 5))


def reference(conductivity, initial_guess, right_side):
    fine_solution, residual_zero = smooth(right_side, initial_guess, conductivity)
    conduct_one = 0.125 * coarse_sum(conductivity)
    level_one_solution, residual_one = smooth(0.25 * coarse_sum(residual_zero), None, conduct_one)
    conduct_two = 0.125 * coarse_sum(conduct_one)
    level_two_solution, residual_two = smooth(0.25 * coarse_sum(residual_one), None, conduct_two)
    conduct_three = 0.125 * coarse_sum(conduct_two)
    level_three_solution, level_three_residual = smooth(0.25 * coarse_sum(residual_two), None, conduct_three)
    return fine_solution, level_one_solution, level_two_solution, level_three_solution, level_three_residual
```

```python
import jax
import jax.numpy as jnp
from jax import lax
from jax.sharding import PartitionSpec as P

SWEEPS = 3

lower_bound = 0.25
upper_bound = 2.0

NEAR = 4
ROWS = 24
COLUMNS = 32


def steps(axis, by):
    count = lax.axis_size(axis)
    forward = [(i, i + by) for i in range(count - by)]
    return forward, [(b, a) for a, b in forward]


def with_halo(block, sides, width):
    for axis, dim in sides:
        forward, backward = steps(axis, 1)
        low = lax.ppermute(
            lax.slice_in_dim(block, block.shape[dim] - width, None, axis=dim), axis, forward
        )
        high = lax.ppermute(lax.slice_in_dim(block, 0, width, axis=dim), axis, backward)
        block = jnp.concatenate([low, block, high], axis=dim)
    return block


def copy_for_each(shard, axis):
    peers = lax.axis_size(axis)
    return lax.all_to_all(
        jnp.broadcast_to(shard[None], (peers, *shard.shape)), axis, 0, 0, tiled=True
    )


def gathered(shard, axis):
    peers = lax.axis_size(axis)
    inner = 4 if peers % 4 == 0 else 1
    outer = peers // inner
    apart = [[i + inner * j for j in range(outer)] for i in range(inner)]
    beside = [[inner * j + i for i in range(inner)] for j in range(outer)]
    for groups in (apart, beside):
        shard = lax.all_to_all(
            jnp.broadcast_to(shard[None], (len(groups[0]), *shard.shape)),
            axis,
            0,
            0,
            axis_index_groups=groups,
            tiled=True,
        )
    return jnp.moveaxis(shard, 0, 1).reshape(peers, *shard.shape[2:])


def inside_mask(shape, sides):
    inside = None
    for axis, dim, own in sides:
        halo = (shape[dim] - own) // 2
        position = lax.axis_index(axis) * own - halo + lax.broadcasted_iota(jnp.int32, shape, dim)
        good = (position >= 0) & (position < lax.axis_size(axis) * own)
        inside = good if inside is None else inside & good
    return inside


def neighbours(padded):
    return [
        padded[:-2, 1:-1, 1:-1],
        padded[2:, 1:-1, 1:-1],
        padded[1:-1, :-2, 1:-1],
        padded[1:-1, 2:, 1:-1],
        padded[1:-1, 1:-1, :-2],
        padded[1:-1, 1:-1, 2:],
    ]


def operate(field, weights, diagonal):
    others = neighbours(jnp.pad(field, 1))
    result = diagonal * field
    for face_index in range(6):
        result = result - weights[face_index] * others[face_index]
    return result


def smooth(source, start, conduct, inside):
    theta = 0.5 * (upper_bound + lower_bound)
    delta = 0.5 * (upper_bound - lower_bound)
    sigma = theta / delta
    others = neighbours(jnp.pad(conduct, 1))
    weights = [0.5 * (conduct + other) for other in others]
    diagonal = weights[0] + weights[1] + weights[2] + weights[3] + weights[4] + weights[5]
    safe_diagonal = jnp.where(inside, diagonal, 1.0)
    if start is None:
        solution = jnp.zeros_like(source)
        residual = source
    else:
        solution = start
        residual = source - operate(solution, weights, diagonal)
    direction = jnp.where(inside, residual / (theta * safe_diagonal), 0.0)
    ratio_now = 1.0 / sigma
    for sweep_index in range(SWEEPS):
        solution = solution + direction
        residual = residual - operate(direction, weights, diagonal)
        if sweep_index + 1 < SWEEPS:
            ratio_next = 1.0 / (2.0 * sigma - ratio_now)
            direction = jnp.where(
                inside,
                ratio_next * ratio_now * direction
                + 2.0 * ratio_next / delta * residual / safe_diagonal,
                0.0,
            )
            ratio_now = ratio_next
    return solution, residual


def pairs(size):
    row = lax.broadcasted_iota(jnp.int32, (size, size // 2), 0)
    column = lax.broadcasted_iota(jnp.int32, (size, size // 2), 1)
    return (row // 2 == column).astype(jnp.float32)


def coarse_sum(field):
    first, second, third = field.shape
    planes = field.reshape(first // 2, 2, second, third)
    planes = planes[:, 0] + planes[:, 1]
    planes = jnp.einsum("xzy,yb->xzb", planes, pairs(third), precision=lax.Precision.HIGHEST)
    return jnp.einsum("xzb,za->xab", planes, pairs(second), precision=lax.Precision.HIGHEST)


def shards(conductivity, initial_guess, right_side):
    grown = with_halo(
        jnp.stack([conductivity, right_side, initial_guess]),
        (("gx", 1), ("gy", 3), ("gz", 2)),
        NEAR,
    )
    inside = inside_mask(
        grown.shape[1:],
        (
            ("gx", 0, conductivity.shape[0]),
            ("gz", 1, conductivity.shape[1]),
            ("gy", 2, conductivity.shape[2]),
        ),
    )
    fine, residual_zero = smooth(grown[1], grown[2], grown[0], inside)
    own = (slice(NEAR, -NEAR),) * 3
    fine_solution = fine[own]

    source = 0.25 * coarse_sum(residual_zero[own])
    conduct = 0.125 * coarse_sum(conductivity)
    planes, rows, columns = source.shape
    packed = jnp.concatenate([source, conduct], axis=2)
    everyone = copy_for_each(packed, "gz")
    everyone = jnp.moveaxis(everyone, 0, 1).reshape(planes, -1, 2 * columns)
    everyone = jnp.pad(everyone, ((0, 0), (ROWS, ROWS), (0, 0)))
    packed = lax.dynamic_slice_in_dim(
        everyone, lax.axis_index("gz") * rows, rows + 2 * ROWS, axis=1
    )
    both = jnp.stack([packed[..., :columns], packed[..., columns:]])
    both = with_halo(both, (("gy", 3),), COLUMNS)
    parts = {0: both}
    for by in (1, 2):
        forward, backward = steps("gx", by)
        parts[-by] = lax.ppermute(both, "gx", forward)
        parts[by] = lax.ppermute(both, "gx", backward)
    both = jnp.concatenate([parts[by] for by in sorted(parts)], axis=1)
    inside = inside_mask(
        both.shape[1:], (("gx", 0, planes), ("gz", 1, rows), ("gy", 2, columns))
    )
    level_one, residual_one = smooth(both[0], None, both[1], inside)
    level_one_solution = level_one[
        2 * planes : -2 * planes, ROWS:-ROWS, COLUMNS:-COLUMNS
    ]

    source = 0.25 * coarse_sum(residual_one[2 * planes : -2 * planes])
    conduct = 0.125 * coarse_sum(both[1, 2 * planes : -2 * planes])
    width = source.shape[2]
    packed = gathered(jnp.concatenate([source, conduct], axis=2)[0], "gx")
    source, conduct = packed[..., :width], packed[..., width:]
    rows, columns = rows // 2, columns // 2
    inside = inside_mask(source.shape, (("gz", 1, rows), ("gy", 2, columns)))
    level_two, residual_two = smooth(source, None, conduct, inside)
    level_two_solution = level_two[:, ROWS // 2 : -ROWS // 2, COLUMNS // 2 : -COLUMNS // 2]

    source = 0.25 * coarse_sum(residual_two)
    conduct = 0.125 * coarse_sum(conduct)
    rows, columns = rows // 2, columns // 2
    inside = inside_mask(source.shape, (("gz", 1, rows), ("gy", 2, columns)))
    level_three, residual_three = smooth(source, None, conduct, inside)
    own = (slice(None), slice(ROWS // 4, -ROWS // 4), slice(COLUMNS // 4, -COLUMNS // 4))
    return (
        fine_solution,
        level_one_solution,
        level_two_solution,
        level_three[own],
        residual_three[own],
    )


def solution(mesh):
    placed = (P("gx", "gz", "gy"), P("gx", "gz", "gy"), P("gx", "gz", "gy"))
    return jax.shard_map(
        shards,
        mesh=mesh,
        in_specs=placed,
        out_specs=(
            P("gx", "gz", "gy"),
            P("gx", "gz", "gy"),
            P(None, "gz", "gy"),
            P(None, "gz", "gy"),
            P(None, "gz", "gy"),
        ),
        check_vma=False,
    )
```

```python
import jax
import jax.numpy as jnp
from jax import lax
from jax.experimental import pallas as pl
from jax.experimental.pallas import tpu as pltpu
from jax.sharding import PartitionSpec as P

SWEEPS = 3

lower_bound = 0.25
upper_bound = 2.0

NEAR = 4
ROWS = 24
COLUMNS = 32


def steps(axis, by):
    count = lax.axis_size(axis)
    forward = [(i, i + by) for i in range(count - by)]
    return forward, [(b, a) for a, b in forward]


def with_halo(block, sides, width):
    for axis, dim in sides:
        forward, backward = steps(axis, 1)
        low = lax.ppermute(
            lax.slice_in_dim(block, block.shape[dim] - width, None, axis=dim), axis, forward
        )
        high = lax.ppermute(lax.slice_in_dim(block, 0, width, axis=dim), axis, backward)
        block = jnp.concatenate([low, block, high], axis=dim)
    return block


def copy_for_each(shard, axis):
    peers = lax.axis_size(axis)
    return lax.all_to_all(
        jnp.broadcast_to(shard[None], (peers, *shard.shape)), axis, 0, 0, tiled=True
    )


def gathered(shard, axis):
    peers = lax.axis_size(axis)
    inner = 4 if peers % 4 == 0 else 1
    outer = peers // inner
    apart = [[i + inner * j for j in range(outer)] for i in range(inner)]
    beside = [[inner * j + i for i in range(inner)] for j in range(outer)]
    for groups in (apart, beside):
        shard = lax.all_to_all(
            jnp.broadcast_to(shard[None], (len(groups[0]), *shard.shape)),
            axis,
            0,
            0,
            axis_index_groups=groups,
            tiled=True,
        )
    return shard


def inside_mask(shape, sides):
    inside = None
    for axis, dim, own in sides:
        halo = (shape[dim] - own) // 2
        position = lax.axis_index(axis) * own - halo + lax.broadcasted_iota(jnp.int32, shape, dim)
        good = (position >= 0) & (position < lax.axis_size(axis) * own)
        inside = good if inside is None else inside & good
    return inside


def neighbours(padded):
    return [
        padded[:-2, 1:-1, 1:-1],
        padded[2:, 1:-1, 1:-1],
        padded[1:-1, :-2, 1:-1],
        padded[1:-1, 2:, 1:-1],
        padded[1:-1, 1:-1, :-2],
        padded[1:-1, 1:-1, 2:],
    ]


def operate(field, weights, diagonal):
    others = neighbours(jnp.pad(field, 1))
    result = diagonal * field
    for face_index in range(6):
        result = result - weights[face_index] * others[face_index]
    return result


def smooth(source, start, conduct, inside):
    theta = 0.5 * (upper_bound + lower_bound)
    delta = 0.5 * (upper_bound - lower_bound)
    sigma = theta / delta
    others = neighbours(jnp.pad(conduct, 1))
    weights = [0.5 * (conduct + other) for other in others]
    diagonal = weights[0] + weights[1] + weights[2] + weights[3] + weights[4] + weights[5]
    safe_diagonal = jnp.where(inside, diagonal, 1.0)
    if start is None:
        solution = jnp.zeros_like(source)
        residual = source
    else:
        solution = start
        residual = source - operate(solution, weights, diagonal)
    direction = jnp.where(inside, residual / (theta * safe_diagonal), 0.0)
    ratio_now = 1.0 / sigma
    for sweep_index in range(SWEEPS):
        solution = solution + direction
        residual = residual - operate(direction, weights, diagonal)
        if sweep_index + 1 < SWEEPS:
            ratio_next = 1.0 / (2.0 * sigma - ratio_now)
            direction = jnp.where(
                inside,
                ratio_next * ratio_now * direction
                + 2.0 * ratio_next / delta * residual / safe_diagonal,
                0.0,
            )
            ratio_now = ratio_next
    return solution, residual


THETA = 0.5 * (upper_bound + lower_bound)
DELTA = 0.5 * (upper_bound - lower_bound)


def mixes():
    sigma = THETA / DELTA
    ratio_now = 1.0 / sigma
    for _ in range(SWEEPS - 1):
        ratio_next = 1.0 / (2.0 * sigma - ratio_now)
        yield ratio_next * ratio_now, 2.0 * ratio_next / DELTA
        ratio_now = ratio_next


def after(plane, dim):
    return pltpu.roll(plane, plane.shape[dim] - 1, dim)


def before(plane, dim):
    return pltpu.roll(plane, 1, dim)


def set_faces(p, c, wx_low, wx_high, wz, wy, inv):
    face_z = 0.5 * (c + after(c, 0))
    face_y = 0.5 * (c + after(c, 1))
    wz[p] = face_z
    wy[p] = face_y
    diagonal = (
        (wx_low + wx_high) + (face_z + before(face_z, 0)) + (face_y + before(face_y, 1))
    )
    inside = c > 0.0
    inverse = jnp.where(inside, 1.0 / jnp.where(inside, diagonal, 1.0), 0.0)
    inv[p] = inverse
    return inverse


def gained(p, here, flow_low, flow_high, wz, wy):
    flow_z = wz[p] * (after(here, 0) - here)
    flow_y = wy[p] * (after(here, 1) - here)
    return (
        (flow_high - flow_low)
        + (flow_z - before(flow_z, 0))
        + (flow_y - before(flow_y, 1))
    )


def pairing(shift):
    row = lax.broadcasted_iota(jnp.int32, (128, 128), 0)
    column = lax.broadcasted_iota(jnp.int32, (128, 128), 1)
    return jnp.where((row >> 1) + shift == column, 1.0, 0.0)


def paired(left, right):
    return jnp.dot(
        left, right, precision=lax.Precision.HIGHEST, preferred_element_type=jnp.float32
    )


def level_one_kernel(
    far_low, low, own, high, far_high, solution_ref, packed_ref, d, r, wx, wz, wy, inv, both
):
    parts = (far_low, low, own, high, far_high)
    planes = own.shape[1]
    total = planes * len(parts)
    first = 2 * planes
    last = first + planes

    def conduct(p):
        return parts[p // planes][1, p % planes]

    def flow(p):
        return wx[p] * (d[p + 1] - d[p])

    reach = SWEEPS
    for p in range(first - reach - 1, last + reach):
        wx[p] = 0.5 * (conduct(p) + conduct(p + 1))
    for p in range(first - reach, last + reach):
        inverse = set_faces(p, conduct(p), wx[p - 1], wx[p], wz, wy, inv)
        source = parts[p // planes][0, p % planes]
        r[p] = source
        d[p] = source * inverse * (1.0 / THETA)
    answers = [d[p] for p in range(first, last)]
    mix = list(mixes())
    for sweep in range(SWEEPS):
        reach -= 1
        flow_low = flow(first - reach - 1)
        for p in range(first - reach, last + reach):
            flow_high = flow(p)
            here = d[p]
            residual = r[p] + gained(p, here, flow_low, flow_high, wz, wy)
            r[p] = residual
            flow_low = flow_high
            if sweep + 1 < SWEEPS:
                here = mix[sweep][0] * here + mix[sweep][1] * (residual * inv[p])
                d[p] = here
                if first <= p < last:
                    answers[p - first] = answers[p - first] + here
    rows, columns = solution_ref.shape[1:]
    for p in range(planes):
        answer = answers[p][ROWS : ROWS + rows]
        solution_ref[p] = pltpu.roll(answer, 128 - COLUMNS, 1)[:, :columns]
    tall = d.shape[1]
    both[:tall] = 0.25 * (r[first] + r[first + 1])
    both[tall:] = 0.125 * (conduct(first) + conduct(first + 1))
    halved = both[pl.ds(0, tall, stride=2)] + both[pl.ds(1, tall, stride=2)]
    packed_ref[...] = paired(halved[: tall // 2], pairing(0)) + paired(
        halved[tall // 2 :], pairing(64)
    )


def smooth_folded(half, c, r, d, s, wx, wz, wy, inv):
    count = c.shape[0]
    lane = lax.broadcasted_iota(jnp.int32, c.shape[1:], 1)

    def ahead(plane):
        return jnp.where(lane < half, pltpu.roll(plane, 128 - half, 1), 0.0)

    def behind(plane):
        return jnp.where((lane >= half) & (lane < 2 * half), pltpu.roll(plane, half, 1), 0.0)

    wx[0] = 0.5 * (behind(c[count - 1]) + c[0])
    for p in range(count):
        there = c[p + 1] if p + 1 < count else ahead(c[0])
        wx[p + 1] = 0.5 * (c[p] + there)
    for p in range(count):
        inverse = set_faces(p, c[p], wx[p], wx[p + 1], wz, wy, inv)
        direction = r[p] * inverse * (1.0 / THETA)
        d[p] = direction
        s[p] = direction
    mix = list(mixes())
    for sweep in range(SWEEPS):
        beyond = ahead(d[0])
        flow_low = wx[0] * (d[0] - behind(d[count - 1]))
        for p in range(count):
            here = d[p]
            there = d[p + 1] if p + 1 < count else beyond
            flow_high = wx[p + 1] * (there - here)
            residual = r[p] + gained(p, here, flow_low, flow_high, wz, wy)
            r[p] = residual
            flow_low = flow_high
            if sweep + 1 < SWEEPS:
                here = mix[sweep][0] * here + mix[sweep][1] * (residual * inv[p])
                d[p] = here
                s[p] = s[p] + here


def unfold(planes, half, row, column, out_ref):
    count = planes.shape[0]
    rows, columns = out_ref.shape[1:]
    for p in range(count):
        answer = planes[p][row : row + rows]
        out_ref[p] = pltpu.roll(answer, 128 - column, 1)[:, :columns]
        out_ref[p + count] = pltpu.roll(answer, 128 - half - column, 1)[:, :columns]


def coarse_kernel(
    gathered_ref,
    two_ref,
    three_ref,
    residual_ref,
    c, r, d, s, wx, wz, wy, inv, both,
    c3, r3, d3, s3, wx3, wz3, wy3, inv3,
):
    inner = gathered_ref.shape[0]
    count = c.shape[0]
    lane = lax.broadcasted_iota(jnp.int32, c.shape[1:], 1)
    for p in range(count):
        front = gathered_ref[p % inner, p // inner]
        back = gathered_ref[(p + count) % inner, (p + count) // inner]
        r[p] = jnp.where(lane < 64, front, pltpu.roll(back, 64, 1))
        c[p] = jnp.where(lane < 64, pltpu.roll(front, 64, 1), back)
    smooth_folded(64, c, r, d, s, wx, wz, wy, inv)
    unfold(s, 64, ROWS // 2, COLUMNS // 2, two_ref)
    tall = c.shape[1]
    half = count // 2
    for p in range(half):
        both[p * tall : (p + 1) * tall] = 0.25 * (r[2 * p] + r[2 * p + 1])
        both[(half + p) * tall : (half + p + 1) * tall] = 0.125 * (c[2 * p] + c[2 * p + 1])
    length = half * tall
    halved = both[pl.ds(0, length, stride=2)] + both[pl.ds(1, length, stride=2)]
    coarse = paired(halved, pairing(0))
    low = tall // 2
    for p in range(half):
        r3[p] = coarse[p * low : (p + 1) * low]
        c3[p] = coarse[(half + p) * low : (half + p + 1) * low]
    smooth_folded(32, c3, r3, d3, s3, wx3, wz3, wy3, inv3)
    unfold(s3, 32, ROWS // 4, COLUMNS // 4, three_ref)
    unfold(r3, 32, ROWS // 4, COLUMNS // 4, residual_ref)


def f32(*shape):
    return jax.ShapeDtypeStruct(shape, jnp.float32)


def in_vmem(count):
    return [pl.BlockSpec(memory_space=pltpu.VMEM)] * count


def level_one_call(parts, rows, columns):
    _, planes, tall, wide = parts[0].shape
    total = planes * len(parts)
    return pl.pallas_call(
        level_one_kernel,
        out_shape=(f32(planes, rows, columns), f32(tall // 2, wide)),
        in_specs=in_vmem(5),
        out_specs=tuple(in_vmem(2)),
        scratch_shapes=[pltpu.VMEM((total, tall, wide), jnp.float32)] * 6
        + [pltpu.VMEM((2 * tall, wide), jnp.float32)],
    )(*parts)


def coarse_call(everyone, rows, columns):
    inner, outer, tall, wide = everyone.shape
    count = inner * outer // 2

    def scratch(planes, height):
        field = pltpu.VMEM((planes, height, wide), jnp.float32)
        faces = pltpu.VMEM((planes + 1, height, wide), jnp.float32)
        return [field] * 4 + [faces] + [field] * 3

    return pl.pallas_call(
        coarse_kernel,
        out_shape=(
            f32(2 * count, rows, columns),
            f32(count, rows // 2, columns // 2),
            f32(count, rows // 2, columns // 2),
        ),
        in_specs=in_vmem(1),
        out_specs=tuple(in_vmem(3)),
        scratch_shapes=scratch(count, tall)
        + [pltpu.VMEM((count * tall, wide), jnp.float32)]
        + scratch(count // 2, tall // 2),
    )(everyone)


def pairs(size):
    row = lax.broadcasted_iota(jnp.int32, (size, size // 2), 0)
    column = lax.broadcasted_iota(jnp.int32, (size, size // 2), 1)
    return (row // 2 == column).astype(jnp.float32)


def coarse_sum(field):
    first, second, third = field.shape
    planes = field.reshape(first // 2, 2, second, third)
    planes = planes[:, 0] + planes[:, 1]
    planes = jnp.einsum("xzy,yb->xzb", planes, pairs(third), precision=lax.Precision.HIGHEST)
    return jnp.einsum("xzb,za->xab", planes, pairs(second), precision=lax.Precision.HIGHEST)


def shards(conductivity, initial_guess, right_side):
    grown = with_halo(
        jnp.stack([conductivity, right_side, initial_guess]),
        (("gx", 1), ("gy", 3), ("gz", 2)),
        NEAR,
    )
    inside = inside_mask(
        grown.shape[1:],
        (
            ("gx", 0, conductivity.shape[0]),
            ("gz", 1, conductivity.shape[1]),
            ("gy", 2, conductivity.shape[2]),
        ),
    )
    fine, residual_zero = smooth(grown[1], grown[2], grown[0], inside)
    own = (slice(NEAR, -NEAR),) * 3
    fine_solution = fine[own]

    source = 0.25 * coarse_sum(residual_zero[own])
    conduct = 0.125 * coarse_sum(conductivity)
    planes, rows, columns = source.shape
    packed = jnp.concatenate([source, conduct], axis=2)
    everyone = copy_for_each(packed, "gz")
    everyone = jnp.moveaxis(everyone, 0, 1).reshape(planes, -1, 2 * columns)
    everyone = jnp.pad(everyone, ((0, 0), (ROWS, ROWS), (0, 0)))
    packed = lax.dynamic_slice_in_dim(
        everyone, lax.axis_index("gz") * rows, rows + 2 * ROWS, axis=1
    )
    both = jnp.stack([packed[..., :columns], packed[..., columns:]])
    both = with_halo(both, (("gy", 3),), COLUMNS)
    parts = {0: both}
    for by in (1, 2):
        forward, backward = steps("gx", by)
        parts[-by] = lax.ppermute(both, "gx", forward)
        parts[by] = lax.ppermute(both, "gx", backward)
    level_one_solution, packed = level_one_call(
        [parts[by] for by in sorted(parts)], rows, columns
    )
    everyone = gathered(packed, "gx")
    level_two_solution, level_three_solution, level_three_residual = coarse_call(
        everyone, rows // 2, columns // 2
    )
    return (
        fine_solution,
        level_one_solution,
        level_two_solution,
        level_three_solution,
        level_three_residual,
    )


def solution(mesh):
    placed = (P("gx", "gz", "gy"), P("gx", "gz", "gy"), P("gx", "gz", "gy"))
    return jax.shard_map(
        shards,
        mesh=mesh,
        in_specs=placed,
        out_specs=(
            P("gx", "gz", "gy"),
            P("gx", "gz", "gy"),
            P(None, "gz", "gy"),
            P(None, "gz", "gy"),
            P(None, "gz", "gy"),
        ),
        check_vma=False,
    )
```

```python
import jax
import jax.numpy as jnp
from jax import lax
from jax.experimental import pallas as pl
from jax.experimental.pallas import tpu as pltpu
from jax.sharding import PartitionSpec as P

SWEEPS = 3

lower_bound = 0.25
upper_bound = 2.0

NEAR = 4
ROWS = 24
COLUMNS = 32
INNER = 4


def steps(axis, by):
    count = lax.axis_size(axis)
    forward = [(i, i + by) for i in range(count - by)]
    return forward, [(b, a) for a, b in forward]


def shifted(low_side, high_side, axis, by=1):
    forward, backward = steps(axis, by)
    return lax.ppermute(low_side, axis, forward), lax.ppermute(high_side, axis, backward)


def near_halo(bundle):
    low, high = shifted(bundle, bundle, "gx")
    parts = (low, bundle, high)

    def joined(pick):
        return jnp.concatenate([pick(part) for part in parts], axis=1)

    left, right = shifted(
        joined(lambda part: part[..., -NEAR:]), joined(lambda part: part[..., :NEAR]), "gy"
    )
    up = jnp.concatenate(
        [left[:, :, -NEAR:], joined(lambda part: part[:, :, -NEAR:]), right[:, :, -NEAR:]], axis=3
    )
    down = jnp.concatenate(
        [left[:, :, :NEAR], joined(lambda part: part[:, :, :NEAR]), right[:, :, :NEAR]], axis=3
    )
    below, above = shifted(up, down, "gz")
    middle = jnp.concatenate([left, joined(lambda part: part), right], axis=3)
    return jnp.concatenate([below, middle, above], axis=2)


def copy_for_each(shard, axis):
    peers = lax.axis_size(axis)
    return lax.all_to_all(
        jnp.broadcast_to(shard[None], (peers, *shard.shape)), axis, 0, 0, tiled=True
    )


def gathered(copies, axis):
    outer = copies.shape[0]
    apart = [[i + INNER * j for j in range(outer)] for i in range(INNER)]
    beside = [[INNER * j + i for i in range(INNER)] for j in range(outer)]
    shard = lax.all_to_all(copies, axis, 0, 0, axis_index_groups=apart, tiled=True)
    copies = jnp.broadcast_to(shard[None], (INNER, *shard.shape))
    return lax.all_to_all(copies, axis, 0, 0, axis_index_groups=beside, tiled=True)


def inside_mask(shape, sides):
    inside = None
    for axis, dim, own in sides:
        halo = (shape[dim] - own) // 2
        position = lax.axis_index(axis) * own - halo + lax.broadcasted_iota(jnp.int32, shape, dim)
        good = (position >= 0) & (position < lax.axis_size(axis) * own)
        inside = good if inside is None else inside & good
    return inside


def neighbours(padded):
    return [
        padded[:-2, 1:-1, 1:-1],
        padded[2:, 1:-1, 1:-1],
        padded[1:-1, :-2, 1:-1],
        padded[1:-1, 2:, 1:-1],
        padded[1:-1, 1:-1, :-2],
        padded[1:-1, 1:-1, 2:],
    ]


def operate(field, weights, diagonal):
    others = neighbours(jnp.pad(field, 1))
    result = diagonal * field
    for face_index in range(6):
        result = result - weights[face_index] * others[face_index]
    return result


def smooth(source, start, conduct, inside):
    theta = 0.5 * (upper_bound + lower_bound)
    delta = 0.5 * (upper_bound - lower_bound)
    sigma = theta / delta
    others = neighbours(jnp.pad(conduct, 1))
    weights = [0.5 * (conduct + other) for other in others]
    diagonal = weights[0] + weights[1] + weights[2] + weights[3] + weights[4] + weights[5]
    safe_diagonal = jnp.where(inside, diagonal, 1.0)
    if start is None:
        solution = jnp.zeros_like(source)
        residual = source
    else:
        solution = start
        residual = source - operate(solution, weights, diagonal)
    direction = jnp.where(inside, residual / (theta * safe_diagonal), 0.0)
    ratio_now = 1.0 / sigma
    for sweep_index in range(SWEEPS):
        solution = solution + direction
        residual = residual - operate(direction, weights, diagonal)
        if sweep_index + 1 < SWEEPS:
            ratio_next = 1.0 / (2.0 * sigma - ratio_now)
            direction = jnp.where(
                inside,
                ratio_next * ratio_now * direction
                + 2.0 * ratio_next / delta * residual / safe_diagonal,
                0.0,
            )
            ratio_now = ratio_next
    return solution, residual


THETA = 0.5 * (upper_bound + lower_bound)
DELTA = 0.5 * (upper_bound - lower_bound)


def mixes():
    sigma = THETA / DELTA
    ratio_now = 1.0 / sigma
    for _ in range(SWEEPS - 1):
        ratio_next = 1.0 / (2.0 * sigma - ratio_now)
        yield ratio_next * ratio_now, 2.0 * ratio_next / DELTA
        ratio_now = ratio_next


def after(plane, dim):
    return pltpu.roll(plane, plane.shape[dim] - 1, dim)


def before(plane, dim):
    return pltpu.roll(plane, 1, dim)


def set_faces(p, c, wx_low, wx_high, wz, wy, inv):
    face_z = 0.5 * (c + after(c, 0))
    face_y = 0.5 * (c + after(c, 1))
    wz[p] = face_z
    wy[p] = face_y
    diagonal = (
        (wx_low + wx_high) + (face_z + before(face_z, 0)) + (face_y + before(face_y, 1))
    )
    inside = c > 0.0
    inverse = jnp.where(inside, 1.0 / jnp.where(inside, diagonal, 1.0), 0.0)
    inv[p] = inverse
    return inverse


def gained(p, here, flow_low, flow_high, wz, wy):
    flow_z = wz[p] * (after(here, 0) - here)
    flow_y = wy[p] * (after(here, 1) - here)
    return (
        (flow_high - flow_low)
        + (flow_z - before(flow_z, 0))
        + (flow_y - before(flow_y, 1))
    )


def pairing(shift):
    row = lax.broadcasted_iota(jnp.int32, (128, 128), 0)
    column = lax.broadcasted_iota(jnp.int32, (128, 128), 1)
    return jnp.where((row >> 1) + shift == column, 1.0, 0.0)


def paired(left, right):
    return jnp.dot(
        left, right, precision=lax.Precision.HIGHEST, preferred_element_type=jnp.float32
    )


def level_one_kernel(
    far_low, low, own, high, far_high, solution_ref, packed_ref, d, r, wx, wz, wy, inv, both
):
    planes = own.shape[0] // 2
    first = 2 * planes
    last = first + planes
    whole = {1: low, 2: own, 3: high}

    def conduct(p):
        if p // planes in whole:
            return whole[p // planes][planes + p % planes]
        return (far_low if p < first else far_high)[1 + p % planes]

    def origin(p):
        if p // planes in whole:
            return whole[p // planes][p % planes]
        return (far_low if p < first else far_high)[0]

    def flow(p):
        return wx[p] * (d[p + 1] - d[p])

    reach = SWEEPS
    for p in range(first - reach - 1, last + reach):
        wx[p] = 0.5 * (conduct(p) + conduct(p + 1))
    for p in range(first - reach, last + reach):
        inverse = set_faces(p, conduct(p), wx[p - 1], wx[p], wz, wy, inv)
        source = origin(p)
        r[p] = source
        d[p] = source * inverse * (1.0 / THETA)
    answers = [d[p] for p in range(first, last)]
    mix = list(mixes())
    for sweep in range(SWEEPS):
        reach -= 1
        flow_low = flow(first - reach - 1)
        for p in range(first - reach, last + reach):
            flow_high = flow(p)
            here = d[p]
            residual = r[p] + gained(p, here, flow_low, flow_high, wz, wy)
            r[p] = residual
            flow_low = flow_high
            if sweep + 1 < SWEEPS:
                here = mix[sweep][0] * here + mix[sweep][1] * (residual * inv[p])
                d[p] = here
                if first <= p < last:
                    answers[p - first] = answers[p - first] + here
    rows, columns = solution_ref.shape[1:]
    for p in range(planes):
        answer = answers[p][ROWS : ROWS + rows]
        solution_ref[p] = pltpu.roll(answer, 128 - COLUMNS, 1)[:, :columns]
    tall = d.shape[1]
    both[:tall] = 0.25 * (r[first] + r[first + 1])
    both[tall:] = 0.125 * (conduct(first) + conduct(first + 1))
    halved = both[pl.ds(0, tall, stride=2)] + both[pl.ds(1, tall, stride=2)]
    packed = paired(halved[: tall // 2], pairing(0)) + paired(halved[tall // 2 :], pairing(64))
    for copy in range(packed_ref.shape[0]):
        packed_ref[copy] = packed


def smooth_folded(half, c, r, d, s, wx, wz, wy, inv):
    count = c.shape[0]
    lane = lax.broadcasted_iota(jnp.int32, c.shape[1:], 1)

    def ahead(plane):
        return jnp.where(lane < half, pltpu.roll(plane, 128 - half, 1), 0.0)

    def behind(plane):
        return jnp.where((lane >= half) & (lane < 2 * half), pltpu.roll(plane, half, 1), 0.0)

    wx[0] = 0.5 * (behind(c[count - 1]) + c[0])
    for p in range(count):
        there = c[p + 1] if p + 1 < count else ahead(c[0])
        wx[p + 1] = 0.5 * (c[p] + there)
    for p in range(count):
        inverse = set_faces(p, c[p], wx[p], wx[p + 1], wz, wy, inv)
        direction = r[p] * inverse * (1.0 / THETA)
        d[p] = direction
        s[p] = direction
    mix = list(mixes())
    for sweep in range(SWEEPS):
        beyond = ahead(d[0])
        flow_low = wx[0] * (d[0] - behind(d[count - 1]))
        for p in range(count):
            here = d[p]
            there = d[p + 1] if p + 1 < count else beyond
            flow_high = wx[p + 1] * (there - here)
            residual = r[p] + gained(p, here, flow_low, flow_high, wz, wy)
            r[p] = residual
            flow_low = flow_high
            if sweep + 1 < SWEEPS:
                here = mix[sweep][0] * here + mix[sweep][1] * (residual * inv[p])
                d[p] = here
                s[p] = s[p] + here


def unfold(planes, half, row, column, out_ref):
    count = planes.shape[0]
    rows, columns = out_ref.shape[1:]
    for p in range(count):
        answer = planes[p][row : row + rows]
        out_ref[p] = pltpu.roll(answer, 128 - column, 1)[:, :columns]
        out_ref[p + count] = pltpu.roll(answer, 128 - half - column, 1)[:, :columns]


def coarse_kernel(
    gathered_ref,
    two_ref,
    three_ref,
    residual_ref,
    c, r, d, s, wx, wz, wy, inv, both,
    c3, r3, d3, s3, wx3, wz3, wy3, inv3,
):
    inner = gathered_ref.shape[0]
    count = c.shape[0]
    lane = lax.broadcasted_iota(jnp.int32, c.shape[1:], 1)
    for p in range(count):
        front = gathered_ref[p % inner, p // inner]
        back = gathered_ref[(p + count) % inner, (p + count) // inner]
        r[p] = jnp.where(lane < 64, front, pltpu.roll(back, 64, 1))
        c[p] = jnp.where(lane < 64, pltpu.roll(front, 64, 1), back)
    smooth_folded(64, c, r, d, s, wx, wz, wy, inv)
    unfold(s, 64, ROWS // 2, COLUMNS // 2, two_ref)
    tall = c.shape[1]
    half = count // 2
    for p in range(half):
        both[p * tall : (p + 1) * tall] = 0.25 * (r[2 * p] + r[2 * p + 1])
        both[(half + p) * tall : (half + p + 1) * tall] = 0.125 * (c[2 * p] + c[2 * p + 1])
    length = half * tall
    halved = both[pl.ds(0, length, stride=2)] + both[pl.ds(1, length, stride=2)]
    coarse = paired(halved, pairing(0))
    low = tall // 2
    for p in range(half):
        r3[p] = coarse[p * low : (p + 1) * low]
        c3[p] = coarse[(half + p) * low : (half + p + 1) * low]
    smooth_folded(32, c3, r3, d3, s3, wx3, wz3, wy3, inv3)
    unfold(s3, 32, ROWS // 4, COLUMNS // 4, three_ref)
    unfold(r3, 32, ROWS // 4, COLUMNS // 4, residual_ref)


def f32(*shape):
    return jax.ShapeDtypeStruct(shape, jnp.float32)


def in_vmem(count):
    return [pl.BlockSpec(memory_space=pltpu.VMEM)] * count


def level_one_call(parts, rows, columns):
    planes, tall, wide = parts[2].shape
    planes //= 2
    total = planes * len(parts)
    return pl.pallas_call(
        level_one_kernel,
        out_shape=(f32(planes, rows, columns), f32(lax.axis_size("gx") // INNER, tall // 2, wide)),
        in_specs=in_vmem(5),
        out_specs=tuple(in_vmem(2)),
        scratch_shapes=[pltpu.VMEM((total, tall, wide), jnp.float32)] * 6
        + [pltpu.VMEM((2 * tall, wide), jnp.float32)],
        compiler_params=pltpu.CompilerParams(vmem_limit_bytes=8 * 2**20),
    )(*parts)


def coarse_call(everyone, rows, columns):
    inner, outer, tall, wide = everyone.shape
    count = inner * outer // 2

    def scratch(planes, height):
        field = pltpu.VMEM((planes, height, wide), jnp.float32)
        faces = pltpu.VMEM((planes + 1, height, wide), jnp.float32)
        return [field] * 4 + [faces] + [field] * 3

    return pl.pallas_call(
        coarse_kernel,
        out_shape=(
            f32(2 * count, rows, columns),
            f32(count, rows // 2, columns // 2),
            f32(count, rows // 2, columns // 2),
        ),
        in_specs=in_vmem(1),
        out_specs=tuple(in_vmem(3)),
        scratch_shapes=scratch(count, tall)
        + [pltpu.VMEM((count * tall, wide), jnp.float32)]
        + scratch(count // 2, tall // 2),
        compiler_params=pltpu.CompilerParams(vmem_limit_bytes=8 * 2**20),
    )(everyone)


def pairs(size):
    row = lax.broadcasted_iota(jnp.int32, (size, size // 2), 0)
    column = lax.broadcasted_iota(jnp.int32, (size, size // 2), 1)
    return (row // 2 == column).astype(jnp.float32)


def coarse_sum(field):
    first, second, third = field.shape
    planes = field.reshape(first // 2, 2, second, third)
    planes = planes[:, 0] + planes[:, 1]
    planes = jnp.einsum("xzy,yb->xzb", planes, pairs(third), precision=lax.Precision.HIGHEST)
    return jnp.einsum("xzb,za->xab", planes, pairs(second), precision=lax.Precision.HIGHEST)


def shards(conductivity, initial_guess, right_side):
    grown = near_halo(jnp.stack([conductivity, right_side, initial_guess]))
    inside = inside_mask(
        grown.shape[1:],
        (
            ("gx", 0, conductivity.shape[0]),
            ("gz", 1, conductivity.shape[1]),
            ("gy", 2, conductivity.shape[2]),
        ),
    )
    fine, residual_zero = smooth(grown[1], grown[2], grown[0], inside)
    own = (slice(NEAR, -NEAR),) * 3
    fine_solution = fine[own]

    source = 0.25 * coarse_sum(residual_zero[own])
    conduct = 0.125 * coarse_sum(conductivity)
    planes, rows, columns = source.shape
    packed = jnp.concatenate([source, conduct], axis=2)
    everyone = copy_for_each(packed, "gz")
    everyone = jnp.moveaxis(everyone, 0, 1).reshape(planes, -1, 2 * columns)
    everyone = jnp.pad(everyone, ((0, 0), (ROWS, ROWS), (0, 0)))
    packed = lax.dynamic_slice_in_dim(
        everyone, lax.axis_index("gz") * rows, rows + 2 * ROWS, axis=1
    )
    pieces = [packed[p, :, q * columns : (q + 1) * columns] for q in (0, 1) for p in range(planes)]
    left, right = shifted(
        jnp.concatenate([piece[:, -COLUMNS:] for piece in pieces], axis=1),
        jnp.concatenate([piece[:, :COLUMNS] for piece in pieces], axis=1),
        "gy",
    )
    pieces = [
        jnp.concatenate(
            [
                left[:, i * COLUMNS : (i + 1) * COLUMNS],
                piece,
                right[:, i * COLUMNS : (i + 1) * COLUMNS],
            ],
            axis=1,
        )
        for i, piece in enumerate(pieces)
    ]
    source, conduct = pieces[:planes], pieces[planes:]
    far = shifted(
        jnp.stack([source[-1], *conduct]), jnp.stack([source[0], *conduct]), "gx", 2
    )
    own = jnp.stack(source + conduct)
    near = shifted(own, own, "gx")
    level_one_solution, packed = level_one_call(
        (far[0], near[0], own, near[1], far[1]), rows, columns
    )
    everyone = gathered(packed, "gx")
    level_two_solution, level_three_solution, level_three_residual = coarse_call(
        everyone, rows // 2, columns // 2
    )
    return (
        fine_solution,
        level_one_solution,
        level_two_solution,
        level_three_solution,
        level_three_residual,
    )


def solution(mesh):
    placed = (P("gx", "gz", "gy"), P("gx", "gz", "gy"), P("gx", "gz", "gy"))
    return jax.shard_map(
        shards,
        mesh=mesh,
        in_specs=placed,
        out_specs=(
            P("gx", "gz", "gy"),
            P("gx", "gz", "gy"),
            P(None, "gz", "gy"),
            P(None, "gz", "gy"),
            P(None, "gz", "gy"),
        ),
        check_vma=False,
    )
```

```python
import jax
import jax.numpy as jnp
from jax import lax
from jax.experimental import pallas as pl
from jax.experimental.pallas import tpu as pltpu
from jax.sharding import PartitionSpec as P

SWEEPS = 3

lower_bound = 0.25
upper_bound = 2.0

NEAR = 4
ROWS = 24
COLUMNS = 32
INNER = 4


def steps(axis, by):
    count = lax.axis_size(axis)
    forward = [(i, i + by) for i in range(count - by)]
    return forward, [(b, a) for a, b in forward]


def shifted(low_side, high_side, axis, by=1):
    forward, backward = steps(axis, by)
    return lax.ppermute(low_side, axis, forward), lax.ppermute(high_side, axis, backward)


def near_halo(bundle):
    low, high = shifted(bundle, bundle, "gx")
    parts = (low, bundle, high)
    below, above = shifted(
        jnp.concatenate([part[:, :, -NEAR:] for part in parts], axis=1),
        jnp.concatenate([part[:, :, :NEAR] for part in parts], axis=1),
        "gz",
    )
    seen = (*parts, below, above)
    right_edge, left_edge = edges_call(seen)
    return (*seen, *shifted(right_edge, left_edge, "gy"))


def gathered(copies, axis):
    outer = copies.shape[0]
    apart = [[i + INNER * j for j in range(outer)] for i in range(INNER)]
    beside = [[INNER * j + i for i in range(INNER)] for j in range(outer)]
    shard = lax.all_to_all(copies, axis, 0, 0, axis_index_groups=apart, tiled=True)
    copies = jnp.broadcast_to(shard[None], (INNER, *shard.shape))
    return lax.all_to_all(copies, axis, 0, 0, axis_index_groups=beside, tiled=True)


THETA = 0.5 * (upper_bound + lower_bound)
DELTA = 0.5 * (upper_bound - lower_bound)


def mixes():
    sigma = THETA / DELTA
    ratio_now = 1.0 / sigma
    for _ in range(SWEEPS - 1):
        ratio_next = 1.0 / (2.0 * sigma - ratio_now)
        yield ratio_next * ratio_now, 2.0 * ratio_next / DELTA
        ratio_now = ratio_next


def after(plane, dim):
    return pltpu.roll(plane, plane.shape[dim] - 1, dim)


def before(plane, dim):
    return pltpu.roll(plane, 1, dim)


def set_faces(p, c, wx_low, wx_high, wz, wy, inv):
    face_z = 0.5 * (c + after(c, 0))
    face_y = 0.5 * (c + after(c, 1))
    wz[p] = face_z
    wy[p] = face_y
    diagonal = (
        (wx_low + wx_high) + (face_z + before(face_z, 0)) + (face_y + before(face_y, 1))
    )
    inside = c > 0.0
    inverse = jnp.where(inside, 1.0 / jnp.where(inside, diagonal, 1.0), 0.0)
    inv[p] = inverse
    return inverse


def gained(p, here, flow_low, flow_high, wz, wy):
    flow_z = wz[p] * (after(here, 0) - here)
    flow_y = wy[p] * (after(here, 1) - here)
    return (
        (flow_high - flow_low)
        + (flow_z - before(flow_z, 0))
        + (flow_y - before(flow_y, 1))
    )


def pairing(shift):
    row = lax.broadcasted_iota(jnp.int32, (128, 128), 0)
    column = lax.broadcasted_iota(jnp.int32, (128, 128), 1)
    return jnp.where((row >> 1) + shift == column, 1.0, 0.0)


def paired(left, right):
    return jnp.dot(
        left, right, precision=lax.Precision.HIGHEST, preferred_element_type=jnp.float32
    )


def fine_tiles(low, own, high, below, above, corner):
    arrays, planes, rows, _ = own.shape
    parts = (low, own, high)
    for a in range(arrays):
        for p in range(planes * len(parts)):
            part = parts[p // planes]
            for row in range(0, rows, 8):
                yield a, p, row, part[a, p % planes, row : row + 8]
            corner[:NEAR] = above[a, p]
            corner[NEAR:] = below[a, p]
            yield a, p, rows, corner[...]


def edges_kernel(low, own, high, below, above, right_edge, left_edge, corner):
    lane = lax.broadcasted_iota(jnp.int32, (8, 128), 1)
    slots = 128 // NEAR
    for t, (_, _, _, tile) in enumerate(fine_tiles(low, own, high, below, above, corner)):
        k = t % slots
        if k == 0:
            right = left = jnp.zeros((8, 128), jnp.float32)
        here = (lane >= NEAR * k) & (lane < NEAR * (k + 1))
        right = jnp.where(here, turned(tile, NEAR * (k + 1)), right)
        left = jnp.where(here, turned(tile, NEAR * k), left)
        place = pl.ds(8 * (t // slots), 8)
        right_edge[place] = right
        left_edge[place] = left


def turned(tile, shift):
    return pltpu.roll(tile, shift % 128, 1) if shift % 128 else tile


def fine_kernel(
    low, own, high, below, above, left, right, solution_ref, packed_ref,
    c, r, u, d, wx, wz, wy, inv, both, corner,
):
    planes, rows = own.shape[1:3]
    first, last = planes, 2 * planes
    lane = lax.broadcasted_iota(jnp.int32, (8, 128), 1)
    slots = 128 // NEAR
    for t, (a, p, row, tile) in enumerate(fine_tiles(low, own, high, below, above, corner)):
        k = t % slots
        place = pl.ds(8 * (t // slots), 8)
        near = jnp.where(lane < NEAR, turned(right[place], -NEAR * k), 0.0)
        near = jnp.where(lane >= 128 - NEAR, turned(left[place], -NEAR * (k + 1)), near)
        field = (c, r, u)[a]
        field[p, row : row + 8, :128] = tile
        field[p, row : row + 8, 128:] = near

    def flow(p, field):
        return wx[p] * (field[p + 1] - field[p])

    reach = SWEEPS
    for p in range(first - reach - 1, last + reach):
        wx[p] = 0.5 * (c[p] + c[p + 1])
    flow_low = flow(first - reach - 1, u)
    for p in range(first - reach, last + reach):
        inverse = set_faces(p, c[p], wx[p - 1], wx[p], wz, wy, inv)
        flow_high = flow(p, u)
        here = u[p]
        residual = r[p] + gained(p, here, flow_low, flow_high, wz, wy)
        r[p] = residual
        flow_low = flow_high
        direction = residual * inverse * (1.0 / THETA)
        d[p] = direction
        if first <= p < last:
            solution_ref[p - first] = here[:rows, :128] + direction[:rows, :128]
    mix = list(mixes())
    for sweep in range(SWEEPS):
        reach -= 1
        flow_low = flow(first - reach - 1, d)
        for p in range(first - reach, last + reach):
            flow_high = flow(p, d)
            here = d[p]
            residual = r[p] + gained(p, here, flow_low, flow_high, wz, wy)
            r[p] = residual
            flow_low = flow_high
            if sweep + 1 < SWEEPS:
                here = mix[sweep][0] * here + mix[sweep][1] * (residual * inv[p])
                d[p] = here
                if first <= p < last:
                    solution_ref[p - first] = solution_ref[p - first] + here[:rows, :128]
    half = planes // 2
    for q in range(half):
        p = first + 2 * q
        both[q * rows : (q + 1) * rows] = 0.25 * (r[p, :rows, :128] + r[p + 1, :rows, :128])
        both[(half + q) * rows : (half + q + 1) * rows] = 0.125 * (
            c[p, :rows, :128] + c[p + 1, :rows, :128]
        )
    length = half * rows
    halved = both[pl.ds(0, length, stride=2)] + both[pl.ds(1, length, stride=2)]
    packed = paired(halved[: length // 2], pairing(0)) + paired(
        halved[length // 2 :], pairing(64)
    )
    low_rows = rows // 2
    for copy in range(packed_ref.shape[0]):
        for q in range(half):
            packed_ref[copy, q] = packed[q * low_rows : (q + 1) * low_rows]


def level_one_kernel(
    far_low, low, own, high, far_high, solution_ref, packed_ref, d, r, wx, wz, wy, inv, both
):
    planes = own.shape[0] // 2
    first = 2 * planes
    last = first + planes
    whole = {1: low, 2: own, 3: high}

    def conduct(p):
        if p // planes in whole:
            return whole[p // planes][planes + p % planes]
        return (far_low if p < first else far_high)[1 + p % planes]

    def origin(p):
        if p // planes in whole:
            return whole[p // planes][p % planes]
        return (far_low if p < first else far_high)[0]

    def flow(p):
        return wx[p] * (d[p + 1] - d[p])

    reach = SWEEPS
    for p in range(first - reach - 1, last + reach):
        wx[p] = 0.5 * (conduct(p) + conduct(p + 1))
    for p in range(first - reach, last + reach):
        inverse = set_faces(p, conduct(p), wx[p - 1], wx[p], wz, wy, inv)
        source = origin(p)
        r[p] = source
        d[p] = source * inverse * (1.0 / THETA)
    answers = [d[p] for p in range(first, last)]
    mix = list(mixes())
    for sweep in range(SWEEPS):
        reach -= 1
        flow_low = flow(first - reach - 1)
        for p in range(first - reach, last + reach):
            flow_high = flow(p)
            here = d[p]
            residual = r[p] + gained(p, here, flow_low, flow_high, wz, wy)
            r[p] = residual
            flow_low = flow_high
            if sweep + 1 < SWEEPS:
                here = mix[sweep][0] * here + mix[sweep][1] * (residual * inv[p])
                d[p] = here
                if first <= p < last:
                    answers[p - first] = answers[p - first] + here
    rows, columns = solution_ref.shape[1:]
    for p in range(planes):
        answer = answers[p][ROWS : ROWS + rows]
        solution_ref[p] = pltpu.roll(answer, 128 - COLUMNS, 1)[:, :columns]
    tall = d.shape[1]
    both[:tall] = 0.25 * (r[first] + r[first + 1])
    both[tall:] = 0.125 * (conduct(first) + conduct(first + 1))
    halved = both[pl.ds(0, tall, stride=2)] + both[pl.ds(1, tall, stride=2)]
    packed = paired(halved[: tall // 2], pairing(0)) + paired(halved[tall // 2 :], pairing(64))
    for copy in range(packed_ref.shape[0]):
        packed_ref[copy] = packed


def smooth_folded(half, c, r, d, s, wx, wz, wy, inv):
    count = c.shape[0]
    lane = lax.broadcasted_iota(jnp.int32, c.shape[1:], 1)

    def ahead(plane):
        return jnp.where(lane < half, pltpu.roll(plane, 128 - half, 1), 0.0)

    def behind(plane):
        return jnp.where((lane >= half) & (lane < 2 * half), pltpu.roll(plane, half, 1), 0.0)

    wx[0] = 0.5 * (behind(c[count - 1]) + c[0])
    for p in range(count):
        there = c[p + 1] if p + 1 < count else ahead(c[0])
        wx[p + 1] = 0.5 * (c[p] + there)
    for p in range(count):
        inverse = set_faces(p, c[p], wx[p], wx[p + 1], wz, wy, inv)
        direction = r[p] * inverse * (1.0 / THETA)
        d[p] = direction
        s[p] = direction
    mix = list(mixes())
    for sweep in range(SWEEPS):
        beyond = ahead(d[0])
        flow_low = wx[0] * (d[0] - behind(d[count - 1]))
        for p in range(count):
            here = d[p]
            there = d[p + 1] if p + 1 < count else beyond
            flow_high = wx[p + 1] * (there - here)
            residual = r[p] + gained(p, here, flow_low, flow_high, wz, wy)
            r[p] = residual
            flow_low = flow_high
            if sweep + 1 < SWEEPS:
                here = mix[sweep][0] * here + mix[sweep][1] * (residual * inv[p])
                d[p] = here
                s[p] = s[p] + here


def unfold(planes, half, row, column, out_ref):
    count = planes.shape[0]
    rows, columns = out_ref.shape[1:]
    for p in range(count):
        answer = planes[p][row : row + rows]
        out_ref[p] = pltpu.roll(answer, 128 - column, 1)[:, :columns]
        out_ref[p + count] = pltpu.roll(answer, 128 - half - column, 1)[:, :columns]


def coarse_kernel(
    gathered_ref,
    two_ref,
    three_ref,
    residual_ref,
    c, r, d, s, wx, wz, wy, inv, both,
    c3, r3, d3, s3, wx3, wz3, wy3, inv3,
):
    inner = gathered_ref.shape[0]
    count = c.shape[0]
    lane = lax.broadcasted_iota(jnp.int32, c.shape[1:], 1)
    for p in range(count):
        front = gathered_ref[p % inner, p // inner]
        back = gathered_ref[(p + count) % inner, (p + count) // inner]
        r[p] = jnp.where(lane < 64, front, pltpu.roll(back, 64, 1))
        c[p] = jnp.where(lane < 64, pltpu.roll(front, 64, 1), back)
    smooth_folded(64, c, r, d, s, wx, wz, wy, inv)
    unfold(s, 64, ROWS // 2, COLUMNS // 2, two_ref)
    tall = c.shape[1]
    half = count // 2
    for p in range(half):
        both[p * tall : (p + 1) * tall] = 0.25 * (r[2 * p] + r[2 * p + 1])
        both[(half + p) * tall : (half + p + 1) * tall] = 0.125 * (c[2 * p] + c[2 * p + 1])
    length = half * tall
    halved = both[pl.ds(0, length, stride=2)] + both[pl.ds(1, length, stride=2)]
    coarse = paired(halved, pairing(0))
    low = tall // 2
    for p in range(half):
        r3[p] = coarse[p * low : (p + 1) * low]
        c3[p] = coarse[(half + p) * low : (half + p + 1) * low]
    smooth_folded(32, c3, r3, d3, s3, wx3, wz3, wy3, inv3)
    unfold(s3, 32, ROWS // 4, COLUMNS // 4, three_ref)
    unfold(r3, 32, ROWS // 4, COLUMNS // 4, residual_ref)


def f32(*shape):
    return jax.ShapeDtypeStruct(shape, jnp.float32)


def in_vmem(count):
    return [pl.BlockSpec(memory_space=pltpu.VMEM)] * count


def tight(mebibytes):
    return pltpu.CompilerParams(vmem_limit_bytes=mebibytes * 2**20)


def edges_call(seen):
    arrays, planes, rows, _ = seen[1].shape
    tiles = arrays * planes * 3 * (rows // 8 + 1)
    edge = f32(-(-tiles * NEAR // 128) * 8, 128)
    return pl.pallas_call(
        edges_kernel,
        out_shape=(edge, edge),
        in_specs=in_vmem(5),
        out_specs=tuple(in_vmem(2)),
        scratch_shapes=[pltpu.VMEM((8, 128), jnp.float32)],
        compiler_params=tight(4),
    )(*seen)


def fine_call(seen, peers):
    _, planes, rows, columns = seen[1].shape
    field = pltpu.VMEM((3 * planes, rows + 2 * NEAR, 2 * columns), jnp.float32)
    return pl.pallas_call(
        fine_kernel,
        out_shape=(
            f32(planes, rows, columns),
            f32(peers, planes // 2, rows // 2, columns),
        ),
        in_specs=in_vmem(7),
        out_specs=tuple(in_vmem(2)),
        scratch_shapes=[field] * 8
        + [
            pltpu.VMEM((planes * rows, columns), jnp.float32),
            pltpu.VMEM((8, 128), jnp.float32),
        ],
        compiler_params=tight(12),
    )(*seen)


def level_one_call(parts, rows, columns):
    planes, tall, wide = parts[2].shape
    planes //= 2
    total = planes * len(parts)
    return pl.pallas_call(
        level_one_kernel,
        out_shape=(f32(planes, rows, columns), f32(lax.axis_size("gx") // INNER, tall // 2, wide)),
        in_specs=in_vmem(5),
        out_specs=tuple(in_vmem(2)),
        scratch_shapes=[pltpu.VMEM((total, tall, wide), jnp.float32)] * 6
        + [pltpu.VMEM((2 * tall, wide), jnp.float32)],
        compiler_params=pltpu.CompilerParams(vmem_limit_bytes=8 * 2**20),
    )(*parts)


def coarse_call(everyone, rows, columns):
    inner, outer, tall, wide = everyone.shape
    count = inner * outer // 2

    def scratch(planes, height):
        field = pltpu.VMEM((planes, height, wide), jnp.float32)
        faces = pltpu.VMEM((planes + 1, height, wide), jnp.float32)
        return [field] * 4 + [faces] + [field] * 3

    return pl.pallas_call(
        coarse_kernel,
        out_shape=(
            f32(2 * count, rows, columns),
            f32(count, rows // 2, columns // 2),
            f32(count, rows // 2, columns // 2),
        ),
        in_specs=in_vmem(1),
        out_specs=tuple(in_vmem(3)),
        scratch_shapes=scratch(count, tall)
        + [pltpu.VMEM((count * tall, wide), jnp.float32)]
        + scratch(count // 2, tall // 2),
        compiler_params=pltpu.CompilerParams(vmem_limit_bytes=8 * 2**20),
    )(everyone)


def shards(conductivity, initial_guess, right_side):
    seen = near_halo(jnp.stack([conductivity, right_side, initial_guess]))
    fine_solution, copies = fine_call(seen, lax.axis_size("gz"))
    planes, rows, columns = copies.shape[1:]
    columns //= 2
    everyone = lax.all_to_all(copies, "gz", 0, 0, tiled=True)
    everyone = jnp.moveaxis(everyone, 0, 1).reshape(planes, -1, 2 * columns)
    everyone = jnp.pad(everyone, ((0, 0), (ROWS, ROWS), (0, 0)))
    packed = lax.dynamic_slice_in_dim(
        everyone, lax.axis_index("gz") * rows, rows + 2 * ROWS, axis=1
    )
    pieces = [packed[p, :, q * columns : (q + 1) * columns] for q in (0, 1) for p in range(planes)]
    left, right = shifted(
        jnp.concatenate([piece[:, -COLUMNS:] for piece in pieces], axis=1),
        jnp.concatenate([piece[:, :COLUMNS] for piece in pieces], axis=1),
        "gy",
    )
    pieces = [
        jnp.concatenate(
            [
                left[:, i * COLUMNS : (i + 1) * COLUMNS],
                piece,
                right[:, i * COLUMNS : (i + 1) * COLUMNS],
            ],
            axis=1,
        )
        for i, piece in enumerate(pieces)
    ]
    source, conduct = pieces[:planes], pieces[planes:]
    far = shifted(
        jnp.stack([source[-1], *conduct]), jnp.stack([source[0], *conduct]), "gx", 2
    )
    own = jnp.stack(source + conduct)
    near = shifted(own, own, "gx")
    level_one_solution, packed = level_one_call(
        (far[0], near[0], own, near[1], far[1]), rows, columns
    )
    everyone = gathered(packed, "gx")
    level_two_solution, level_three_solution, level_three_residual = coarse_call(
        everyone, rows // 2, columns // 2
    )
    return (
        fine_solution,
        level_one_solution,
        level_two_solution,
        level_three_solution,
        level_three_residual,
    )


def solution(mesh):
    placed = (P("gx", "gz", "gy"), P("gx", "gz", "gy"), P("gx", "gz", "gy"))
    return jax.shard_map(
        shards,
        mesh=mesh,
        in_specs=placed,
        out_specs=(
            P("gx", "gz", "gy"),
            P("gx", "gz", "gy"),
            P(None, "gz", "gy"),
            P(None, "gz", "gy"),
            P(None, "gz", "gy"),
        ),
        check_vma=False,
    )
```

```python
import jax
import jax.numpy as jnp
from jax import lax
from jax.experimental import pallas as pl
from jax.experimental.pallas import tpu as pltpu
from jax.sharding import PartitionSpec as P

SWEEPS = 3

lower_bound = 0.25
upper_bound = 2.0

NEAR = 4
ROWS = 24
COLUMNS = 32
REACH = 10
SKIP = ROWS // 2 - REACH
EDGE = COLUMNS // 2 - REACH


def steps(axis, by):
    count = lax.axis_size(axis)
    forward = [(i, i + by) for i in range(count - by)]
    return forward, [(b, a) for a, b in forward]


def around(axis, by):
    count = lax.axis_size(axis)
    forward = [(i, (i + by) % count) for i in range(count)]
    return forward, [(b, a) for a, b in forward]


def shifted(low_side, high_side, axis, by=1):
    forward, backward = around(axis, by) if axis == "gx" else steps(axis, by)
    return lax.ppermute(low_side, axis, forward), lax.ppermute(high_side, axis, backward)


def near_halo(bundle):
    low, high = shifted(bundle, bundle, "gx")
    parts = (low, bundle, high)
    below, above = shifted(
        jnp.concatenate([part[:, :, -NEAR:] for part in parts], axis=1),
        jnp.concatenate([part[:, :, :NEAR] for part in parts], axis=1),
        "gz",
    )
    seen = (*parts, below, above)
    right_edge, left_edge = edges_call(seen)
    return (*seen, *shifted(right_edge, left_edge, "gy"))


def gathered(copies, axis):
    outer = copies.shape[0]
    apart = [[i + 2 * j for j in range(outer)] for i in range(2)]
    mine = lax.all_to_all(copies, axis, 0, 0, axis_index_groups=apart, tiled=True)
    return mine, lax.ppermute(mine, axis, [(i, i ^ 1) for i in range(2 * outer)])


THETA = 0.5 * (upper_bound + lower_bound)
DELTA = 0.5 * (upper_bound - lower_bound)


def mixes():
    sigma = THETA / DELTA
    ratio_now = 1.0 / sigma
    for _ in range(SWEEPS - 1):
        ratio_next = 1.0 / (2.0 * sigma - ratio_now)
        yield ratio_next * ratio_now, 2.0 * ratio_next / DELTA
        ratio_now = ratio_next


def after(plane, dim):
    return pltpu.roll(plane, plane.shape[dim] - 1, dim)


def before(plane, dim):
    return pltpu.roll(plane, 1, dim)


def set_faces(p, c, wx_low, wx_high, wz, wy, inv):
    face_z = 0.5 * (c + after(c, 0))
    face_y = 0.5 * (c + after(c, 1))
    wz[p] = face_z
    wy[p] = face_y
    diagonal = (
        (wx_low + wx_high) + (face_z + before(face_z, 0)) + (face_y + before(face_y, 1))
    )
    inside = c > 0.0
    inverse = jnp.where(inside, 1.0 / jnp.where(inside, diagonal, 1.0), 0.0)
    inv[p] = inverse
    return inverse


def gained(p, here, flow_low, flow_high, wz, wy):
    flow_z = wz[p] * (after(here, 0) - here)
    flow_y = wy[p] * (after(here, 1) - here)
    return (
        (flow_high - flow_low)
        + (flow_z - before(flow_z, 0))
        + (flow_y - before(flow_y, 1))
    )


def pairing(shift, skip=0):
    half = lax.broadcasted_iota(jnp.int32, (128, 128), 0) >> 1
    column = lax.broadcasted_iota(jnp.int32, (128, 128), 1)
    kept = (half >= skip) & (half < 64 - skip) & (half + shift - skip == column)
    return jnp.where(kept, 1.0, 0.0)


def turned(tile, shift):
    return pltpu.roll(tile, shift % 128, 1) if shift % 128 else tile


def message_shape(rows):
    wide = 64 - 2 * EDGE
    spare = 128 - 2 * wide
    kept = rows - 2 * SKIP
    body = kept // 8 * 8
    pieces = -(-2 * wide // spare)
    assert pieces * (kept - body) <= body
    return wide, spare, kept, body, pieces


def paired(left, right):
    return jnp.dot(
        left, right, precision=lax.Precision.HIGHEST, preferred_element_type=jnp.float32
    )


def fine_tiles(low, own, high, below, above, corner):
    arrays, planes, rows, _ = own.shape
    parts = (low, own, high)
    for a in range(arrays):
        for p in range(planes * len(parts)):
            part = parts[p // planes]
            for row in range(0, rows, 8):
                yield a, p, row, part[a, p % planes, row : row + 8]
            corner[:NEAR] = above[a, p]
            corner[NEAR:] = below[a, p]
            yield a, p, rows, corner[...]


def exists(step):
    index = lax.axis_index("gx") + step
    return (index >= 0) & (index < lax.axis_size("gx"))


def edges_kernel(low, own, high, below, above, right_edge, left_edge, corner):
    lane = lax.broadcasted_iota(jnp.int32, (8, 128), 1)
    slots = 128 // NEAR
    for t, (_, _, _, tile) in enumerate(fine_tiles(low, own, high, below, above, corner)):
        k = t % slots
        if k == 0:
            right = left = jnp.zeros((8, 128), jnp.float32)
        here = (lane >= NEAR * k) & (lane < NEAR * (k + 1))
        right = jnp.where(here, turned(tile, NEAR * (k + 1)), right)
        left = jnp.where(here, turned(tile, NEAR * k), left)
        place = pl.ds(8 * (t // slots), 8)
        right_edge[place] = right
        left_edge[place] = left


def fine_kernel(
    low, own, high, below, above, left, right, solution_ref, packed_ref,
    c, r, u, d, wx, wz, wy, inv, both, corner,
):
    planes, rows = own.shape[1:3]
    first, last = planes, 2 * planes
    lane = lax.broadcasted_iota(jnp.int32, (8, 128), 1)
    slots = 128 // NEAR
    for t, (a, p, row, tile) in enumerate(fine_tiles(low, own, high, below, above, corner)):
        k = t % slots
        place = pl.ds(8 * (t // slots), 8)
        near = jnp.where(lane < NEAR, turned(right[place], -NEAR * k), 0.0)
        near = jnp.where(lane >= 128 - NEAR, turned(left[place], -NEAR * (k + 1)), near)
        if p // planes != 1 and a != 1:
            valid = exists(p // planes - 1)
            tile = jnp.where(valid, tile, 0.0)
            near = jnp.where(valid, near, 0.0)
        field = (c, r, u)[a]
        field[p, row : row + 8, :128] = tile
        field[p, row : row + 8, 128:] = near

    def flow(p, field):
        return wx[p] * (field[p + 1] - field[p])

    reach = SWEEPS
    for p in range(first - reach - 1, last + reach):
        wx[p] = 0.5 * (c[p] + c[p + 1])
    flow_low = flow(first - reach - 1, u)
    for p in range(first - reach, last + reach):
        inverse = set_faces(p, c[p], wx[p - 1], wx[p], wz, wy, inv)
        flow_high = flow(p, u)
        here = u[p]
        residual = r[p] + gained(p, here, flow_low, flow_high, wz, wy)
        r[p] = residual
        flow_low = flow_high
        direction = residual * inverse * (1.0 / THETA)
        d[p] = direction
        if first <= p < last:
            solution_ref[p - first] = here[:rows, :128] + direction[:rows, :128]
    mix = list(mixes())
    for sweep in range(SWEEPS):
        reach -= 1
        flow_low = flow(first - reach - 1, d)
        for p in range(first - reach, last + reach):
            flow_high = flow(p, d)
            here = d[p]
            residual = r[p] + gained(p, here, flow_low, flow_high, wz, wy)
            r[p] = residual
            flow_low = flow_high
            if sweep + 1 < SWEEPS:
                here = mix[sweep][0] * here + mix[sweep][1] * (residual * inv[p])
                d[p] = here
                if first <= p < last:
                    solution_ref[p - first] = solution_ref[p - first] + here[:rows, :128]
    half = planes // 2
    for q in range(half):
        p = first + 2 * q
        both[q * rows : (q + 1) * rows] = 0.25 * (r[p, :rows, :128] + r[p + 1, :rows, :128])
        both[(half + q) * rows : (half + q + 1) * rows] = 0.125 * (
            c[p, :rows, :128] + c[p + 1, :rows, :128]
        )
    length = half * rows
    halved = both[pl.ds(0, length, stride=2)] + both[pl.ds(1, length, stride=2)]
    packed = paired(halved[: length // 2], pairing(0)) + paired(
        halved[length // 2 :], pairing(64)
    )
    low_rows = rows // 2
    for copy in range(packed_ref.shape[0]):
        for q in range(half):
            packed_ref[copy, q] = packed[q * low_rows : (q + 1) * low_rows]


def level_one_kernel(
    far_low, low, own, high, far_high, solution_ref, packed_ref, d, r, wx, wz, wy, inv, both
):
    planes = own.shape[0] // 2
    first = 2 * planes
    last = first + planes
    whole = {1: low, 2: own, 3: high}

    def conduct(p):
        if p // planes in whole:
            plane = whole[p // planes][planes + p % planes]
        else:
            plane = (far_low if p < first else far_high)[1 + p % planes]
        step = p // planes - 2
        return jnp.where(exists(step), plane, 0.0) if step else plane

    def origin(p):
        if p // planes in whole:
            return whole[p // planes][p % planes]
        return (far_low if p < first else far_high)[0]

    def flow(p):
        return wx[p] * (d[p + 1] - d[p])

    reach = SWEEPS
    for p in range(first - reach - 1, last + reach):
        wx[p] = 0.5 * (conduct(p) + conduct(p + 1))
    for p in range(first - reach, last + reach):
        inverse = set_faces(p, conduct(p), wx[p - 1], wx[p], wz, wy, inv)
        source = origin(p)
        r[p] = source
        d[p] = source * inverse * (1.0 / THETA)
    answers = [d[p] for p in range(first, last)]
    mix = list(mixes())
    for sweep in range(SWEEPS):
        reach -= 1
        flow_low = flow(first - reach - 1)
        for p in range(first - reach, last + reach):
            flow_high = flow(p)
            here = d[p]
            residual = r[p] + gained(p, here, flow_low, flow_high, wz, wy)
            r[p] = residual
            flow_low = flow_high
            if sweep + 1 < SWEEPS:
                here = mix[sweep][0] * here + mix[sweep][1] * (residual * inv[p])
                d[p] = here
                if first <= p < last:
                    answers[p - first] = answers[p - first] + here
    rows, columns = solution_ref.shape[1:]
    for p in range(planes):
        answer = answers[p][ROWS : ROWS + rows]
        solution_ref[p] = pltpu.roll(answer, 128 - COLUMNS, 1)[:, :columns]
    tall = d.shape[1]
    both[:tall] = 0.25 * (r[first] + r[first + 1])
    both[tall:] = 0.125 * (conduct(first) + conduct(first + 1))
    halved = both[pl.ds(0, tall, stride=2)] + both[pl.ds(1, tall, stride=2)]
    tall //= 2
    wide, spare, kept, body, pieces = message_shape(tall)
    both[:tall] = paired(halved[:tall], pairing(0, EDGE)) + paired(
        halved[tall:], pairing(wide, EDGE)
    )
    rest = both[SKIP + body : SKIP + kept]
    tail = 2 * tall
    both[tail : tail + body] = jnp.zeros((body, 128), jnp.float32)
    for k in range(pieces):
        place = tail + k * (kept - body)
        both[place : place + kept - body] = turned(rest, 2 * wide - spare * k)
    lane = lax.broadcasted_iota(jnp.int32, (body, 128), 1)
    packed = jnp.where(lane < 2 * wide, both[SKIP : SKIP + body], both[tail : tail + body])
    for copy in range(packed_ref.shape[0]):
        packed_ref[copy] = packed


def smooth_folded(half, c, r, d, s, wx, wz, wy, inv):
    count = c.shape[0]
    lane = lax.broadcasted_iota(jnp.int32, c.shape[1:], 1)

    def ahead(plane):
        return jnp.where(lane < half, pltpu.roll(plane, 128 - half, 1), 0.0)

    def behind(plane):
        return jnp.where((lane >= half) & (lane < 2 * half), pltpu.roll(plane, half, 1), 0.0)

    wx[0] = 0.5 * (behind(c[count - 1]) + c[0])
    for p in range(count):
        there = c[p + 1] if p + 1 < count else ahead(c[0])
        wx[p + 1] = 0.5 * (c[p] + there)
    for p in range(count):
        inverse = set_faces(p, c[p], wx[p], wx[p + 1], wz, wy, inv)
        direction = r[p] * inverse * (1.0 / THETA)
        d[p] = direction
        s[p] = direction
    mix = list(mixes())
    for sweep in range(SWEEPS):
        beyond = ahead(d[0])
        flow_low = wx[0] * (d[0] - behind(d[count - 1]))
        for p in range(count):
            here = d[p]
            there = d[p + 1] if p + 1 < count else beyond
            flow_high = wx[p + 1] * (there - here)
            residual = r[p] + gained(p, here, flow_low, flow_high, wz, wy)
            r[p] = residual
            flow_low = flow_high
            if sweep + 1 < SWEEPS:
                here = mix[sweep][0] * here + mix[sweep][1] * (residual * inv[p])
                d[p] = here
                s[p] = s[p] + here


def unfold(planes, half, row, column, out_ref):
    count = planes.shape[0]
    rows, columns = out_ref.shape[1:]
    for p in range(count):
        answer = planes[p][row : row + rows]
        out_ref[p] = pltpu.roll(answer, 128 - column, 1)[:, :columns]
        out_ref[p + count] = pltpu.roll(answer, 128 - half - column, 1)[:, :columns]


def coarse_kernel(
    mine,
    other,
    two_ref,
    three_ref,
    residual_ref,
    c, r, d, s, wx, wz, wy, inv, both,
    c3, r3, d3, s3, wx3, wz3, wy3, inv3,
):
    count = c.shape[0]
    even = (lax.axis_index("gx") & 1) == 0

    def message(x):
        first, second = mine[x // 2], other[x // 2]
        return jnp.where(even if x % 2 == 0 else ~even, first, second)

    wide, spare, kept, body, pieces = message_shape(c.shape[1])

    def spread(p, place, front, back):
        lane = lax.broadcasted_iota(jnp.int32, front.shape, 1)
        inside = (lane & 63) < wide
        conduct = jnp.where(lane < 64, turned(front, -wide), turned(back, 64 - wide))
        r[p, place] = jnp.where(lane < 64, front, turned(back, 64))
        c[p, place] = jnp.where(inside, conduct, 0.0)

    def rest(message):
        rows = kept - body
        lane = lax.broadcasted_iota(jnp.int32, (rows, 128), 1)
        found = jnp.zeros((rows, 128), jnp.float32)
        for k in range(pieces):
            piece = turned(message[k * rows : (k + 1) * rows], spare * k - 2 * wide)
            found = jnp.where((lane >= spare * k) & (lane < spare * (k + 1)), piece, found)
        return found

    edge = jnp.zeros((SKIP, 128), jnp.float32)
    for p in range(count):
        front, back = message(p), message(p + count)
        for field in (r, c):
            field[p, :SKIP] = edge
            field[p, SKIP + kept :] = edge
        spread(p, slice(SKIP, SKIP + body), front, back)
        spread(p, slice(SKIP + body, SKIP + kept), rest(front), rest(back))
    smooth_folded(64, c, r, d, s, wx, wz, wy, inv)
    unfold(s, 64, ROWS // 2, REACH, two_ref)
    tall = c.shape[1]
    half = count // 2
    for p in range(half):
        both[p * tall : (p + 1) * tall] = 0.25 * (r[2 * p] + r[2 * p + 1])
        both[(half + p) * tall : (half + p + 1) * tall] = 0.125 * (c[2 * p] + c[2 * p + 1])
    length = half * tall
    halved = both[pl.ds(0, length, stride=2)] + both[pl.ds(1, length, stride=2)]
    coarse = paired(halved, pairing(0))
    low = tall // 2
    for p in range(half):
        r3[p] = coarse[p * low : (p + 1) * low]
        c3[p] = coarse[(half + p) * low : (half + p + 1) * low]
    smooth_folded(32, c3, r3, d3, s3, wx3, wz3, wy3, inv3)
    unfold(s3, 32, ROWS // 4, REACH // 2, three_ref)
    unfold(r3, 32, ROWS // 4, REACH // 2, residual_ref)


def f32(*shape):
    return jax.ShapeDtypeStruct(shape, jnp.float32)


def in_vmem(count):
    return [pl.BlockSpec(memory_space=pltpu.VMEM)] * count


def tight(mebibytes):
    return pltpu.CompilerParams(vmem_limit_bytes=mebibytes * 2**20)


def edges_call(seen):
    arrays, planes, rows, _ = seen[1].shape
    tiles = arrays * planes * 3 * (rows // 8 + 1)
    edge = f32(-(-tiles * NEAR // 128) * 8, 128)
    return pl.pallas_call(
        edges_kernel,
        out_shape=(edge, edge),
        in_specs=in_vmem(5),
        out_specs=tuple(in_vmem(2)),
        scratch_shapes=[pltpu.VMEM((8, 128), jnp.float32)],
        compiler_params=tight(4),
    )(*seen)


def fine_call(seen, peers):
    _, planes, rows, columns = seen[1].shape
    field = pltpu.VMEM((3 * planes, rows + 2 * NEAR, 2 * columns), jnp.float32)
    return pl.pallas_call(
        fine_kernel,
        out_shape=(
            f32(planes, rows, columns),
            f32(peers, planes // 2, rows // 2, columns),
        ),
        in_specs=in_vmem(7),
        out_specs=tuple(in_vmem(2)),
        scratch_shapes=[field] * 8
        + [
            pltpu.VMEM((planes * rows, columns), jnp.float32),
            pltpu.VMEM((8, 128), jnp.float32),
        ],
        compiler_params=tight(12),
    )(*seen)


def level_one_call(parts, rows, columns):
    planes, tall, wide = parts[2].shape
    planes //= 2
    total = planes * len(parts)
    return pl.pallas_call(
        level_one_kernel,
        out_shape=(f32(planes, rows, columns), f32(lax.axis_size("gx") // 2, message_shape(tall // 2)[3], wide)),
        in_specs=in_vmem(5),
        out_specs=tuple(in_vmem(2)),
        scratch_shapes=[pltpu.VMEM((total, tall, wide), jnp.float32)] * 6
        + [pltpu.VMEM((2 * tall, wide), jnp.float32)],
        compiler_params=pltpu.CompilerParams(vmem_limit_bytes=8 * 2**20),
    )(*parts)


def coarse_call(halves, rows, columns):
    count, _, wide = halves[0].shape
    tall = rows + ROWS

    def scratch(planes, height):
        field = pltpu.VMEM((planes, height, wide), jnp.float32)
        faces = pltpu.VMEM((planes + 1, height, wide), jnp.float32)
        return [field] * 4 + [faces] + [field] * 3

    return pl.pallas_call(
        coarse_kernel,
        out_shape=(
            f32(2 * count, rows, columns),
            f32(count, rows // 2, columns // 2),
            f32(count, rows // 2, columns // 2),
        ),
        in_specs=in_vmem(2),
        out_specs=tuple(in_vmem(3)),
        scratch_shapes=scratch(count, tall)
        + [pltpu.VMEM((count * tall, wide), jnp.float32)]
        + scratch(count // 2, tall // 2),
        compiler_params=pltpu.CompilerParams(vmem_limit_bytes=8 * 2**20),
    )(*halves)


def shards(conductivity, initial_guess, right_side):
    seen = near_halo(jnp.stack([conductivity, right_side, initial_guess]))
    rows = conductivity.shape[1] // 2
    row, *seen = lax.optimization_barrier(((lax.axis_index("gz") * rows).astype(jnp.uint32), *seen))
    fine_solution, copies = fine_call(seen, lax.axis_size("gz"))
    planes, rows, columns = copies.shape[1:]
    columns //= 2
    everyone = lax.all_to_all(copies, "gz", 0, 0, tiled=True)
    everyone = jnp.moveaxis(everyone, 0, 1).reshape(planes, -1, 2 * columns)
    everyone = jnp.pad(everyone, ((0, 0), (ROWS, ROWS), (0, 0)))
    packed = lax.dynamic_slice_in_dim(everyone, row, rows + 2 * ROWS, axis=1)
    pieces = [packed[p, :, q * columns : (q + 1) * columns] for q in (0, 1) for p in range(planes)]
    left, right = shifted(
        jnp.concatenate([piece[:, -COLUMNS:] for piece in pieces], axis=1),
        jnp.concatenate([piece[:, :COLUMNS] for piece in pieces], axis=1),
        "gy",
    )
    pieces = [
        jnp.concatenate(
            [
                left[:, i * COLUMNS : (i + 1) * COLUMNS],
                piece,
                right[:, i * COLUMNS : (i + 1) * COLUMNS],
            ],
            axis=1,
        )
        for i, piece in enumerate(pieces)
    ]
    source, conduct = pieces[:planes], pieces[planes:]
    far = shifted(
        jnp.stack([source[-1], *conduct]), jnp.stack([source[0], *conduct]), "gx", 2
    )
    own = jnp.stack(source + conduct)
    near = shifted(own, own, "gx")
    level_one_solution, packed = level_one_call(
        (far[0], near[0], own, near[1], far[1]), rows, columns
    )
    halves = gathered(packed, "gx")
    level_two_solution, level_three_solution, level_three_residual = coarse_call(
        halves, rows // 2, columns // 2
    )
    return (
        fine_solution,
        level_one_solution,
        level_two_solution,
        level_three_solution,
        level_three_residual,
    )


def solution(mesh):
    placed = (P("gx", "gz", "gy"), P("gx", "gz", "gy"), P("gx", "gz", "gy"))
    return jax.shard_map(
        shards,
        mesh=mesh,
        in_specs=placed,
        out_specs=(
            P("gx", "gz", "gy"),
            P("gx", "gz", "gy"),
            P(None, "gz", "gy"),
            P(None, "gz", "gy"),
            P(None, "gz", "gy"),
        ),
        check_vma=False,
    )
```

```python
import jax
import jax.numpy as jnp
from jax import lax
from jax.experimental import pallas as pl
from jax.experimental.pallas import tpu as pltpu
from jax.sharding import PartitionSpec as P

SWEEPS = 3

lower_bound = 0.25
upper_bound = 2.0

NEAR = 4
ROWS = 24
COLUMNS = 32
REACH = 10
SKIP = ROWS // 2 - REACH
EDGE = COLUMNS // 2 - REACH


def around(axis, by):
    count = lax.axis_size(axis)
    forward = [(i, (i + by) % count) for i in range(count)]
    return forward, [(b, a) for a, b in forward]


def shifted(low_side, high_side, axis, by=1):
    forward, backward = around(axis, by)
    return lax.ppermute(low_side, axis, forward), lax.ppermute(high_side, axis, backward)


def near_halo(bundle):
    low, high = shifted(bundle, bundle, "gx")
    parts = (low, bundle, high)
    below, above = shifted(
        jnp.concatenate([part[:, :, -NEAR:] for part in parts], axis=1),
        jnp.concatenate([part[:, :, :NEAR] for part in parts], axis=1),
        "gz",
    )
    seen = (*parts, below, above)
    right_edge, left_edge = edges_call(seen)
    return (*seen, *shifted(right_edge, left_edge, "gy"))


def gathered(copies, axis):
    outer = copies.shape[0]
    apart = [[i + 2 * j for j in range(outer)] for i in range(2)]
    mine = lax.all_to_all(copies, axis, 0, 0, axis_index_groups=apart, tiled=True)
    return mine, lax.ppermute(mine, axis, [(i, i ^ 1) for i in range(2 * outer)])


THETA = 0.5 * (upper_bound + lower_bound)
DELTA = 0.5 * (upper_bound - lower_bound)


def mixes():
    sigma = THETA / DELTA
    ratio_now = 1.0 / sigma
    for _ in range(SWEEPS - 1):
        ratio_next = 1.0 / (2.0 * sigma - ratio_now)
        yield ratio_next * ratio_now, 2.0 * ratio_next / DELTA
        ratio_now = ratio_next


def after(plane, dim):
    return pltpu.roll(plane, plane.shape[dim] - 1, dim)


def before(plane, dim):
    return pltpu.roll(plane, 1, dim)


def set_faces(p, c, wx_low, wx_high, wz, wy, inv):
    face_z = 0.5 * (c + after(c, 0))
    face_y = 0.5 * (c + after(c, 1))
    wz[p] = face_z
    wy[p] = face_y
    diagonal = (
        (wx_low + wx_high) + (face_z + before(face_z, 0)) + (face_y + before(face_y, 1))
    )
    inside = c > 0.0
    inverse = jnp.where(inside, 1.0 / jnp.where(inside, diagonal, 1.0), 0.0)
    inv[p] = inverse
    return inverse


def gained(p, here, flow_low, flow_high, wz, wy):
    flow_z = wz[p] * (after(here, 0) - here)
    flow_y = wy[p] * (after(here, 1) - here)
    return (
        (flow_high - flow_low)
        + (flow_z - before(flow_z, 0))
        + (flow_y - before(flow_y, 1))
    )


def pairing(shift, skip=0):
    half = lax.broadcasted_iota(jnp.int32, (128, 128), 0) >> 1
    column = lax.broadcasted_iota(jnp.int32, (128, 128), 1)
    kept = (half >= skip) & (half < 64 - skip) & (half + shift - skip == column)
    return jnp.where(kept, 1.0, 0.0)


def turned(tile, shift):
    return pltpu.roll(tile, shift % 128, 1) if shift % 128 else tile


def message_shape(rows):
    wide = 64 - 2 * EDGE
    spare = 128 - 2 * wide
    kept = rows - 2 * SKIP
    body = kept // 8 * 8
    pieces = -(-2 * wide // spare)
    assert pieces * (kept - body) <= body
    return wide, spare, kept, body, pieces


def paired(left, right):
    return jnp.dot(
        left, right, precision=lax.Precision.HIGHEST, preferred_element_type=jnp.float32
    )


def fine_tiles(low, own, high, below, above, corner):
    arrays, planes, rows, _ = own.shape
    parts = (low, own, high)
    for a in range(arrays):
        for p in range(planes * len(parts)):
            part = parts[p // planes]
            for row in range(0, rows, 8):
                yield a, p, row, part[a, p % planes, row : row + 8]
            corner[:NEAR] = jnp.where(exists(1, "gz"), above[a, p], 0.0)
            corner[NEAR:] = jnp.where(exists(-1, "gz"), below[a, p], 0.0)
            yield a, p, rows, corner[...]


def exists(step, axis="gx"):
    index = lax.axis_index(axis) + step
    return (index >= 0) & (index < lax.axis_size(axis))


def edges_kernel(low, own, high, below, above, right_edge, left_edge, corner):
    lane = lax.broadcasted_iota(jnp.int32, (8, 128), 1)
    slots = 128 // NEAR
    for t, (_, _, _, tile) in enumerate(fine_tiles(low, own, high, below, above, corner)):
        k = t % slots
        if k == 0:
            right = left = jnp.zeros((8, 128), jnp.float32)
        here = (lane >= NEAR * k) & (lane < NEAR * (k + 1))
        right = jnp.where(here, turned(tile, NEAR * (k + 1)), right)
        left = jnp.where(here, turned(tile, NEAR * k), left)
        place = pl.ds(8 * (t // slots), 8)
        right_edge[place] = right
        left_edge[place] = left


def fine_kernel(
    low, own, high, below, above, left, right, solution_ref, packed_ref,
    c, r, u, d, wx, wz, wy, inv, both, corner,
):
    planes, rows = own.shape[1:3]
    first, last = planes, 2 * planes
    lane = lax.broadcasted_iota(jnp.int32, (8, 128), 1)
    slots = 128 // NEAR
    for t, (a, p, row, tile) in enumerate(fine_tiles(low, own, high, below, above, corner)):
        k = t % slots
        place = pl.ds(8 * (t // slots), 8)
        near = jnp.where((lane < NEAR) & exists(1, "gy"), turned(right[place], -NEAR * k), 0.0)
        near = jnp.where(
            (lane >= 128 - NEAR) & exists(-1, "gy"), turned(left[place], -NEAR * (k + 1)), near
        )
        if p // planes != 1 and a != 1:
            valid = exists(p // planes - 1)
            tile = jnp.where(valid, tile, 0.0)
            near = jnp.where(valid, near, 0.0)
        field = (c, r, u)[a]
        field[p, row : row + 8, :128] = tile
        field[p, row : row + 8, 128:] = near

    def flow(p, field):
        return wx[p] * (field[p + 1] - field[p])

    reach = SWEEPS
    for p in range(first - reach - 1, last + reach):
        wx[p] = 0.5 * (c[p] + c[p + 1])
    flow_low = flow(first - reach - 1, u)
    for p in range(first - reach, last + reach):
        inverse = set_faces(p, c[p], wx[p - 1], wx[p], wz, wy, inv)
        flow_high = flow(p, u)
        here = u[p]
        residual = r[p] + gained(p, here, flow_low, flow_high, wz, wy)
        r[p] = residual
        flow_low = flow_high
        direction = residual * inverse * (1.0 / THETA)
        d[p] = direction
        if first <= p < last:
            solution_ref[p - first] = here[:rows, :128] + direction[:rows, :128]
    mix = list(mixes())
    for sweep in range(SWEEPS):
        reach -= 1
        flow_low = flow(first - reach - 1, d)
        for p in range(first - reach, last + reach):
            flow_high = flow(p, d)
            here = d[p]
            residual = r[p] + gained(p, here, flow_low, flow_high, wz, wy)
            r[p] = residual
            flow_low = flow_high
            if sweep + 1 < SWEEPS:
                here = mix[sweep][0] * here + mix[sweep][1] * (residual * inv[p])
                d[p] = here
                if first <= p < last:
                    solution_ref[p - first] = solution_ref[p - first] + here[:rows, :128]
    half = planes // 2
    for q in range(half):
        p = first + 2 * q
        both[q * rows : (q + 1) * rows] = 0.25 * (r[p, :rows, :128] + r[p + 1, :rows, :128])
        both[(half + q) * rows : (half + q + 1) * rows] = 0.125 * (
            c[p, :rows, :128] + c[p + 1, :rows, :128]
        )
    length = half * rows
    halved = both[pl.ds(0, length, stride=2)] + both[pl.ds(1, length, stride=2)]
    packed = paired(halved[: length // 2], pairing(0)) + paired(
        halved[length // 2 :], pairing(64)
    )
    low_rows = rows // 2
    for copy in range(packed_ref.shape[0]):
        for q in range(half):
            packed_ref[copy, q] = packed[q * low_rows : (q + 1) * low_rows]


def level_one_kernel(
    far_low, low, own, high, far_high, solution_ref, packed_ref, d, r, wx, wz, wy, inv, both
):
    planes = own.shape[0] // 2
    first = 2 * planes
    last = first + planes
    whole = {1: low, 2: own, 3: high}

    def conduct(p):
        if p // planes in whole:
            plane = whole[p // planes][planes + p % planes]
        else:
            plane = (far_low if p < first else far_high)[1 + p % planes]
        step = p // planes - 2
        return jnp.where(exists(step), plane, 0.0) if step else plane

    def origin(p):
        if p // planes in whole:
            return whole[p // planes][p % planes]
        return (far_low if p < first else far_high)[0]

    def flow(p):
        return wx[p] * (d[p + 1] - d[p])

    reach = SWEEPS
    for p in range(first - reach - 1, last + reach):
        wx[p] = 0.5 * (conduct(p) + conduct(p + 1))
    for p in range(first - reach, last + reach):
        inverse = set_faces(p, conduct(p), wx[p - 1], wx[p], wz, wy, inv)
        source = origin(p)
        r[p] = source
        d[p] = source * inverse * (1.0 / THETA)
    answers = [d[p] for p in range(first, last)]
    mix = list(mixes())
    for sweep in range(SWEEPS):
        reach -= 1
        flow_low = flow(first - reach - 1)
        for p in range(first - reach, last + reach):
            flow_high = flow(p)
            here = d[p]
            residual = r[p] + gained(p, here, flow_low, flow_high, wz, wy)
            r[p] = residual
            flow_low = flow_high
            if sweep + 1 < SWEEPS:
                here = mix[sweep][0] * here + mix[sweep][1] * (residual * inv[p])
                d[p] = here
                if first <= p < last:
                    answers[p - first] = answers[p - first] + here
    rows, columns = solution_ref.shape[1:]
    for p in range(planes):
        answer = answers[p][ROWS : ROWS + rows]
        solution_ref[p] = pltpu.roll(answer, 128 - COLUMNS, 1)[:, :columns]
    tall = d.shape[1]
    both[:tall] = 0.25 * (r[first] + r[first + 1])
    both[tall:] = 0.125 * (conduct(first) + conduct(first + 1))
    halved = both[pl.ds(0, tall, stride=2)] + both[pl.ds(1, tall, stride=2)]
    tall //= 2
    wide, spare, kept, body, pieces = message_shape(tall)
    both[:tall] = paired(halved[:tall], pairing(0, EDGE)) + paired(
        halved[tall:], pairing(wide, EDGE)
    )
    rest = both[SKIP + body : SKIP + kept]
    tail = 2 * tall
    both[tail : tail + body] = jnp.zeros((body, 128), jnp.float32)
    for k in range(pieces):
        place = tail + k * (kept - body)
        both[place : place + kept - body] = turned(rest, 2 * wide - spare * k)
    lane = lax.broadcasted_iota(jnp.int32, (body, 128), 1)
    packed = jnp.where(lane < 2 * wide, both[SKIP : SKIP + body], both[tail : tail + body])
    for copy in range(packed_ref.shape[0]):
        packed_ref[copy] = packed


def smooth_folded(half, c, r, d, s, wx, wz, wy, inv):
    count = c.shape[0]
    lane = lax.broadcasted_iota(jnp.int32, c.shape[1:], 1)

    def ahead(plane):
        return jnp.where(lane < half, pltpu.roll(plane, 128 - half, 1), 0.0)

    def behind(plane):
        return jnp.where((lane >= half) & (lane < 2 * half), pltpu.roll(plane, half, 1), 0.0)

    wx[0] = 0.5 * (behind(c[count - 1]) + c[0])
    for p in range(count):
        there = c[p + 1] if p + 1 < count else ahead(c[0])
        wx[p + 1] = 0.5 * (c[p] + there)
    for p in range(count):
        inverse = set_faces(p, c[p], wx[p], wx[p + 1], wz, wy, inv)
        direction = r[p] * inverse * (1.0 / THETA)
        d[p] = direction
        s[p] = direction
    mix = list(mixes())
    for sweep in range(SWEEPS):
        beyond = ahead(d[0])
        flow_low = wx[0] * (d[0] - behind(d[count - 1]))
        for p in range(count):
            here = d[p]
            there = d[p + 1] if p + 1 < count else beyond
            flow_high = wx[p + 1] * (there - here)
            residual = r[p] + gained(p, here, flow_low, flow_high, wz, wy)
            r[p] = residual
            flow_low = flow_high
            if sweep + 1 < SWEEPS:
                here = mix[sweep][0] * here + mix[sweep][1] * (residual * inv[p])
                d[p] = here
                s[p] = s[p] + here


def unfold(planes, half, row, column, out_ref):
    count = planes.shape[0]
    rows, columns = out_ref.shape[1:]
    for p in range(count):
        answer = planes[p][row : row + rows]
        out_ref[p] = pltpu.roll(answer, 128 - column, 1)[:, :columns]
        out_ref[p + count] = pltpu.roll(answer, 128 - half - column, 1)[:, :columns]


def coarse_kernel(
    mine,
    other,
    two_ref,
    three_ref,
    residual_ref,
    c, r, d, s, wx, wz, wy, inv, both,
    c3, r3, d3, s3, wx3, wz3, wy3, inv3,
):
    count = c.shape[0]
    even = (lax.axis_index("gx") & 1) == 0

    def message(x):
        first, second = mine[x // 2], other[x // 2]
        return jnp.where(even if x % 2 == 0 else ~even, first, second)

    wide, spare, kept, body, pieces = message_shape(c.shape[1])

    def spread(p, place, front, back):
        lane = lax.broadcasted_iota(jnp.int32, front.shape, 1)
        inside = (lane & 63) < wide
        conduct = jnp.where(lane < 64, turned(front, -wide), turned(back, 64 - wide))
        r[p, place] = jnp.where(lane < 64, front, turned(back, 64))
        c[p, place] = jnp.where(inside, conduct, 0.0)

    def rest(message):
        rows = kept - body
        lane = lax.broadcasted_iota(jnp.int32, (rows, 128), 1)
        found = jnp.zeros((rows, 128), jnp.float32)
        for k in range(pieces):
            piece = turned(message[k * rows : (k + 1) * rows], spare * k - 2 * wide)
            found = jnp.where((lane >= spare * k) & (lane < spare * (k + 1)), piece, found)
        return found

    edge = jnp.zeros((SKIP, 128), jnp.float32)
    for p in range(count):
        front, back = message(p), message(p + count)
        for field in (r, c):
            field[p, :SKIP] = edge
            field[p, SKIP + kept :] = edge
        spread(p, slice(SKIP, SKIP + body), front, back)
        spread(p, slice(SKIP + body, SKIP + kept), rest(front), rest(back))
    smooth_folded(64, c, r, d, s, wx, wz, wy, inv)
    unfold(s, 64, ROWS // 2, REACH, two_ref)
    tall = c.shape[1]
    half = count // 2
    for p in range(half):
        both[p * tall : (p + 1) * tall] = 0.25 * (r[2 * p] + r[2 * p + 1])
        both[(half + p) * tall : (half + p + 1) * tall] = 0.125 * (c[2 * p] + c[2 * p + 1])
    length = half * tall
    halved = both[pl.ds(0, length, stride=2)] + both[pl.ds(1, length, stride=2)]
    coarse = paired(halved, pairing(0))
    low = tall // 2
    for p in range(half):
        r3[p] = coarse[p * low : (p + 1) * low]
        c3[p] = coarse[(half + p) * low : (half + p + 1) * low]
    smooth_folded(32, c3, r3, d3, s3, wx3, wz3, wy3, inv3)
    unfold(s3, 32, ROWS // 4, REACH // 2, three_ref)
    unfold(r3, 32, ROWS // 4, REACH // 2, residual_ref)


def f32(*shape):
    return jax.ShapeDtypeStruct(shape, jnp.float32)


def in_vmem(count):
    return [pl.BlockSpec(memory_space=pltpu.VMEM)] * count


def tight(mebibytes):
    return pltpu.CompilerParams(vmem_limit_bytes=mebibytes * 2**20)


def edges_call(seen):
    arrays, planes, rows, _ = seen[1].shape
    tiles = arrays * planes * 3 * (rows // 8 + 1)
    edge = f32(-(-tiles * NEAR // 128) * 8, 128)
    return pl.pallas_call(
        edges_kernel,
        out_shape=(edge, edge),
        in_specs=in_vmem(5),
        out_specs=tuple(in_vmem(2)),
        scratch_shapes=[pltpu.VMEM((8, 128), jnp.float32)],
        compiler_params=tight(4),
    )(*seen)


def fine_call(seen, peers):
    _, planes, rows, columns = seen[1].shape
    field = pltpu.VMEM((3 * planes, rows + 2 * NEAR, 2 * columns), jnp.float32)
    return pl.pallas_call(
        fine_kernel,
        out_shape=(
            f32(planes, rows, columns),
            f32(peers, planes // 2, rows // 2, columns),
        ),
        in_specs=in_vmem(7),
        out_specs=tuple(in_vmem(2)),
        scratch_shapes=[field] * 8
        + [
            pltpu.VMEM((planes * rows, columns), jnp.float32),
            pltpu.VMEM((8, 128), jnp.float32),
        ],
        compiler_params=tight(12),
    )(*seen)


def level_one_call(parts, rows, columns):
    planes, tall, wide = parts[2].shape
    planes //= 2
    total = planes * len(parts)
    return pl.pallas_call(
        level_one_kernel,
        out_shape=(f32(planes, rows, columns), f32(lax.axis_size("gx") // 2, message_shape(tall // 2)[3], wide)),
        in_specs=in_vmem(5),
        out_specs=tuple(in_vmem(2)),
        scratch_shapes=[pltpu.VMEM((total, tall, wide), jnp.float32)] * 6
        + [pltpu.VMEM((2 * tall, wide), jnp.float32)],
        compiler_params=pltpu.CompilerParams(vmem_limit_bytes=8 * 2**20),
    )(*parts)


def coarse_call(halves, rows, columns):
    count, _, wide = halves[0].shape
    tall = rows + ROWS

    def scratch(planes, height):
        field = pltpu.VMEM((planes, height, wide), jnp.float32)
        faces = pltpu.VMEM((planes + 1, height, wide), jnp.float32)
        return [field] * 4 + [faces] + [field] * 3

    return pl.pallas_call(
        coarse_kernel,
        out_shape=(
            f32(2 * count, rows, columns),
            f32(count, rows // 2, columns // 2),
            f32(count, rows // 2, columns // 2),
        ),
        in_specs=in_vmem(2),
        out_specs=tuple(in_vmem(3)),
        scratch_shapes=scratch(count, tall)
        + [pltpu.VMEM((count * tall, wide), jnp.float32)]
        + scratch(count // 2, tall // 2),
        compiler_params=pltpu.CompilerParams(vmem_limit_bytes=8 * 2**20),
    )(*halves)


def shards(conductivity, initial_guess, right_side):
    seen = near_halo(jnp.stack([conductivity, right_side, initial_guess]))
    rows = conductivity.shape[1] // 2
    row, *seen = lax.optimization_barrier(((lax.axis_index("gz") * rows).astype(jnp.uint32), *seen))
    fine_solution, copies = fine_call(seen, lax.axis_size("gz"))
    planes, rows, columns = copies.shape[1:]
    columns //= 2
    everyone = lax.all_to_all(copies, "gz", 0, 0, tiled=True)
    everyone = jnp.moveaxis(everyone, 0, 1).reshape(planes, -1, 2 * columns)
    everyone = jnp.pad(everyone, ((0, 0), (ROWS, ROWS), (0, 0)))
    packed = lax.dynamic_slice_in_dim(everyone, row, rows + 2 * ROWS, axis=1)
    pieces = [packed[p, :, q * columns : (q + 1) * columns] for q in (0, 1) for p in range(planes)]
    left, right = shifted(
        jnp.concatenate([piece[:, -COLUMNS:] for piece in pieces], axis=1),
        jnp.concatenate([piece[:, :COLUMNS] for piece in pieces], axis=1),
        "gy",
    )
    left = jnp.where(exists(-1, "gy"), left, 0.0)
    right = jnp.where(exists(1, "gy"), right, 0.0)
    pieces = [
        jnp.concatenate(
            [
                left[:, i * COLUMNS : (i + 1) * COLUMNS],
                piece,
                right[:, i * COLUMNS : (i + 1) * COLUMNS],
            ],
            axis=1,
        )
        for i, piece in enumerate(pieces)
    ]
    source, conduct = pieces[:planes], pieces[planes:]
    far = shifted(
        jnp.stack([source[-1], *conduct]), jnp.stack([source[0], *conduct]), "gx", 2
    )
    own = jnp.stack(source + conduct)
    near = shifted(own, own, "gx")
    level_one_solution, packed = level_one_call(
        (far[0], near[0], own, near[1], far[1]), rows, columns
    )
    halves = gathered(packed, "gx")
    level_two_solution, level_three_solution, level_three_residual = coarse_call(
        halves, rows // 2, columns // 2
    )
    return (
        fine_solution,
        level_one_solution,
        level_two_solution,
        level_three_solution,
        level_three_residual,
    )


def solution(mesh):
    placed = (P("gx", "gz", "gy"), P("gx", "gz", "gy"), P("gx", "gz", "gy"))
    return jax.shard_map(
        shards,
        mesh=mesh,
        in_specs=placed,
        out_specs=(
            P("gx", "gz", "gy"),
            P("gx", "gz", "gy"),
            P(None, "gz", "gy"),
            P(None, "gz", "gy"),
            P(None, "gz", "gy"),
        ),
        check_vma=False,
    )
```
